128 devices in a mesh: gz: 4 (over z_hi, core), gy: 32 (over y, z_lo, x).
Axes of the slice: x: 4, y: 4, z: 4 (z_hi: 2, z_lo: 2; z = z_hi * 2 + z_lo), core: 2. Of those that a mesh axis runs over, the one named last changes fastest.
Arguments:
- velocity: float32 [3, 256, 256, 512], P(None, None, 'gy', 'gz'), may hold values from -0.3 to 0.3
- increment: float32 [3, 256, 256, 512], P(None, None, 'gy', 'gz'), may hold values from -4 to 4
- template: bfloat16 [256, 256, 512], P(None, 'gy', 'gz'), may hold values from 0 to 1
- deformed: bfloat16 [256, 256, 512], P(None, 'gy', 'gz'), may hold values from 0 to 1
Outputs:
- preconditioned: float32 [3, 256, 256, 512], P(None, None, 'gy', 'gz')
The draws below stay inside these ranges and needn't reach their ends.
All inputs are finite; a program needn't handle non-finite values.
Results may differ from the reference program's by a relative error of at most 0.0003.
Values sent between devices are 32-bit elements; how exact they have to be, the bound alone decides.
A program may use at most 256 MiB of HBM per device.

```python
import math
import jax
import jax.numpy as jnp
from jax import lax

NX = 256
NY = 256
NZ = 512


def block_scale(stream_key, shape, shards, least, high):
    def one(axis_at, parts):
        steps = jax.random.uniform(jax.random.fold_in(jax.random.fold_in(stream_key, 6), axis_at), (parts,), jnp.float32, least / len(shards), high / len(shards))
        return jnp.repeat(jnp.exp(steps), shape[axis_at] // parts).reshape((-1,) + (1,) * (len(shape) - axis_at - 1))

    level = one(*shards[0])
    for cut in shards[1:]:
        level = level * one(*cut)
    return level


def bell_draw(stream_key, shape, scale, most, split=(), kind=jnp.bfloat16):
    drawn = jax.random.normal(stream_key, shape, jnp.float32) * scale
    if len(split) > 0:
        drawn = block_scale(stream_key, shape, split, -0.22, 0.18) * drawn
    return jnp.clip(drawn, min=-most, max=most).astype(kind)


def setup_inputs(seed: int = 0) -> dict:
    key_of = jax.random.split(jax.random.key(seed), 5)
    return {
        "velocity": jnp.clip(jax.random.uniform(key_of[0], (3, NX, NY, NZ), jnp.float32, -0.3, 0.3) * block_scale(key_of[0], (3, NX, NY, NZ), ((2, 32), (3, 4)), -0.4, 0.0), -0.3, 0.3),
        "increment": bell_draw(key_of[1], (3, NX, NY, NZ), 1.0, 4.0, ((2, 32), (3, 4)), jnp.float32),
        "template": jnp.clip(1.0 * jax.random.uniform(key_of[2], (NX, NY, NZ), jnp.float32) ** block_scale(key_of[2], (NX, NY, NZ), ((1, 32), (2, 4)), -0.2, 0.2), 0.0, 1.0).astype(jnp.bfloat16),
        "deformed": jnp.clip(1.0 * jax.random.uniform(key_of[3], (NX, NY, NZ), jnp.float32) ** block_scale(key_of[3], (NX, NY, NZ), ((1, 32), (2, 4)), -0.2, 0.2), 0.0, 1.0).astype(jnp.bfloat16),
    }


STEP = 0.5
BETA = 0.02
GAMMA = 0.05
COARSE_BETA = 0.025
OMEGA = 1.0 / (0.05 + 42.0 * 0.02)


def cas_table(count):
    index = jnp.arange(count, dtype=jnp.int32)
    product = (index[:, None] * index[None, :]) % count
    angle = product.astype(jnp.float32) * (2.0 * math.pi / count)
    return jnp.cos(angle) + jnp.sin(angle)


def eigen_line(count):
    index = jnp.arange(count, dtype=jnp.int32).astype(jnp.float32)
    return 2.0 - 2.0 * jnp.cos(index * (2.0 * math.pi / count))


def filtered(field, gamma, beta, inverse):
    nx, ny, nz = field.shape[1], field.shape[2], field.shape[3]
    table_x, table_y, table_z = cas_table(nx), cas_table(ny), cas_table(nz)
    total = eigen_line(nx)[:, None, None] + eigen_line(ny)[None, :, None] + eigen_line(nz)[None, None, :]
    symbol = gamma + beta * total * total
    high = lax.Precision.HIGHEST

    def one(part):
        coeffs = jnp.einsum('xi,ijk->xjk', table_x, part, precision=high)
        coeffs = jnp.einsum('yj,xjk->xyk', table_y, coeffs, precision=high)
        coeffs = jnp.einsum('zk,xyk->xyz', table_z, coeffs, precision=high)
        if inverse:
            coeffs = coeffs / symbol
        else:
            coeffs = coeffs * symbol
        coeffs = jnp.einsum('xi,ijk->xjk', table_x, coeffs, precision=high)
        coeffs = jnp.einsum('yj,xjk->xyk', table_y, coeffs, precision=high)
        coeffs = jnp.einsum('zk,xyk->xyz', table_z, coeffs, precision=high)
        return coeffs / float(nx * ny * nz)

    return lax.map(one, field)


def plus(field, axis):
    return jnp.roll(field, -1, axis)


def minus(field, axis):
    return jnp.roll(field, 1, axis)


def expand(field):
    return jnp.repeat(jnp.repeat(jnp.repeat(field, 4, axis=1), 4, axis=2), 4, axis=3)


def reference(velocity, increment, template, deformed):
    first = template.astype(jnp.float32)
    second = deformed.astype(jnp.float32)
    grad_first = [0.5 * (plus(first, d) - minus(first, d)) for d in range(3)]
    grad_second = [0.5 * (plus(second, d) - minus(second, d)) for d in range(3)]
    state_one = -STEP * (increment[0] * grad_first[0] + increment[1] * grad_first[1] + increment[2] * grad_first[2])
    advect = jnp.zeros_like(state_one)
    for d in range(3):
        advect = advect + jnp.maximum(velocity[d], 0.0) * (state_one - minus(state_one, d))
        advect = advect + jnp.minimum(velocity[d], 0.0) * (plus(state_one, d) - state_one)
    source = increment[0] * grad_second[0] + increment[1] * grad_second[1] + increment[2] * grad_second[2]
    state_two = state_one - STEP * (advect + source)
    adjoint_two = -state_two
    change = jnp.zeros_like(adjoint_two)
    for d in range(3):
        outflow = jnp.maximum(velocity[d], 0.0) * adjoint_two
        inflow = jnp.minimum(velocity[d], 0.0) * adjoint_two
        change = change + (inflow - minus(inflow, d)) + (plus(outflow, d) - outflow)
    adjoint_one = adjoint_two + STEP * change
    force = jnp.stack([STEP * (adjoint_one * grad_first[d] + adjoint_two * grad_second[d]) for d in range(3)])
    hessian = filtered(increment, GAMMA, BETA, False) + force
    nx, ny, nz = hessian.shape[1], hessian.shape[2], hessian.shape[3]
    restricted = jnp.mean(hessian.reshape(3, nx // 4, 4, ny // 4, 4, nz // 4, 4), axis=(2, 4, 6))
    coarse = filtered(restricted, GAMMA, COARSE_BETA, True)
    return expand(coarse) + OMEGA * (hessian - expand(restricted))
```

```python
import math

import jax
import jax.numpy as jnp
from jax import lax
from jax.sharding import PartitionSpec as P

STEP = 0.5
BETA = 0.02
GAMMA = 0.05
COARSE_BETA = 0.025
OMEGA = 1.0 / (0.05 + 42.0 * 0.02)


def extended(cells, sides, width):
    for axis, dim in sides:
        count = lax.axis_size(axis)
        head = lax.slice_in_dim(cells, 0, width, axis=dim)
        tail = lax.slice_in_dim(cells, cells.shape[dim] - width, cells.shape[dim], axis=dim)
        cells = jnp.concatenate(
            [
                lax.ppermute(tail, axis, [(i, (i + 1) % count) for i in range(count)]),
                cells,
                lax.ppermute(head, axis, [((i + 1) % count, i) for i in range(count)]),
            ],
            axis=dim,
        )
    return cells


def shifted(value, axis, by):
    peers = lax.axis_size(axis)
    return lax.ppermute(value, axis, [(i, (i + by) % peers) for i in range(peers)])


def cas_table(count):
    index = jnp.arange(count, dtype=jnp.int32)
    product = index[:, None] * index[None, :] % count
    angle = product.astype(jnp.float32) * (2.0 * math.pi / count)
    return jnp.cos(angle) + jnp.sin(angle)


def eigen_line(count):
    index = jnp.arange(count, dtype=jnp.int32).astype(jnp.float32)
    return 2.0 - 2.0 * jnp.cos(index * (2.0 * math.pi / count))


def with_rims(stacked):
    padded = extended(stacked, (("gy", 2),), 1)
    center = padded[:, :, 1:-1, :]
    first_plane = center[:, :, :, :1]
    last_plane = center[:, :, :, -1:]
    before_plane = shifted(last_plane, "gz", 1)
    after_plane = shifted(first_plane, "gz", -1)
    z_next = jnp.concatenate([center[:, :, :, 1:], after_plane], axis=3)
    z_prev = jnp.concatenate([before_plane, center[:, :, :, :-1]], axis=3)
    pairs = [
        (jnp.roll(center, -1, 1), jnp.roll(center, 1, 1)),
        (padded[:, :, 2:, :], padded[:, :, :-2, :]),
        (z_next, z_prev),
    ]
    return (center, pairs)


def expand(field):
    return jnp.repeat(jnp.repeat(jnp.repeat(field, 4, axis=1), 4, axis=2), 4, axis=3)


def fine_filter(field):
    padded = extended(field, (("gy", 2), ("gz", 3)), 2)
    padded = jnp.concatenate([padded[:, -2:], padded, padded[:, :2]], axis=1)

    def negative_laplacian(cells):
        center = cells[:, 1:-1, 1:-1, 1:-1]
        return (
            6.0 * center
            - (cells[:, 2:, 1:-1, 1:-1] + cells[:, :-2, 1:-1, 1:-1])
            - (cells[:, 1:-1, 2:, 1:-1] + cells[:, 1:-1, :-2, 1:-1])
            - (cells[:, 1:-1, 1:-1, 2:] + cells[:, 1:-1, 1:-1, :-2])
        )

    return GAMMA * field + BETA * negative_laplacian(negative_laplacian(padded))


def coarse_spread(restricted):
    high = lax.Precision.HIGHEST
    groups_z = lax.axis_size("gz")
    groups_y = lax.axis_size("gy")
    cxlen, cylen, czlen = (restricted.shape[1], restricted.shape[2], restricted.shape[3])
    full_y = groups_y * cylen
    full_z = groups_z * czlen
    xpart = cxlen // groups_y
    ypart = full_y // groups_z
    table_x = cas_table(cxlen)
    table_y = cas_table(full_y)
    table_z = cas_table(full_z)
    coeffs = jnp.einsum("xi,cijk->cxjk", table_x, restricted, precision=high)
    rows = lax.all_to_all(coeffs, "gy", split_axis=1, concat_axis=2, tiled=True)
    rows = jnp.einsum("yj,cxjk->cxyk", table_y, rows, precision=high)
    cols = lax.all_to_all(rows, "gz", split_axis=2, concat_axis=3, tiled=True)
    cols = jnp.einsum("zk,cxyk->cxyz", table_z, cols, precision=high)
    line_x = lax.dynamic_slice_in_dim(eigen_line(cxlen), lax.axis_index("gy") * xpart, xpart, 0)
    line_y = lax.dynamic_slice_in_dim(eigen_line(full_y), lax.axis_index("gz") * ypart, ypart, 0)
    total = line_x[:, None, None] + line_y[None, :, None] + eigen_line(full_z)[None, None, :]
    cols = cols / (GAMMA + COARSE_BETA * total * total)
    cols = jnp.einsum("zk,cxyk->cxyz", table_z, cols, precision=high)
    rows = lax.all_to_all(cols, "gz", split_axis=3, concat_axis=2, tiled=True)
    rows = jnp.einsum("yj,cxjk->cxyk", table_y, rows, precision=high)
    coeffs = lax.all_to_all(rows, "gy", split_axis=2, concat_axis=1, tiled=True)
    coeffs = jnp.einsum("xi,cijk->cxjk", table_x, coeffs, precision=high)
    return coeffs / float(cxlen * full_y * full_z)


def per_device(velocity, increment, template, deformed):
    stacked = jnp.concatenate(
        [template.astype(jnp.float32)[None], deformed.astype(jnp.float32)[None], velocity], axis=0
    )
    center, pairs = with_rims(stacked)
    grad_first = [0.5 * (pairs[d][0][0] - pairs[d][1][0]) for d in range(3)]
    grad_second = [0.5 * (pairs[d][0][1] - pairs[d][1][1]) for d in range(3)]
    speed = [center[2 + d] for d in range(3)]
    speed_next = [pairs[d][0][2 + d] for d in range(3)]
    speed_prev = [pairs[d][1][2 + d] for d in range(3)]
    state_one = -STEP * (
        increment[0] * grad_first[0] + increment[1] * grad_first[1] + increment[2] * grad_first[2]
    )
    state_center, state_pairs = with_rims(state_one[None])
    advect = jnp.zeros_like(state_one)
    for d in range(3):
        advect = advect + jnp.maximum(speed[d], 0.0) * (state_center[0] - state_pairs[d][1][0])
        advect = advect + jnp.minimum(speed[d], 0.0) * (state_pairs[d][0][0] - state_center[0])
    source = (
        increment[0] * grad_second[0]
        + increment[1] * grad_second[1]
        + increment[2] * grad_second[2]
    )
    state_two = state_one - STEP * (advect + source)
    adjoint_two = -state_two
    adjoint_center, adjoint_pairs = with_rims(adjoint_two[None])
    change = jnp.zeros_like(adjoint_two)
    for d in range(3):
        inflow = jnp.minimum(speed[d], 0.0) * adjoint_two
        inflow_prev = jnp.minimum(speed_prev[d], 0.0) * adjoint_pairs[d][1][0]
        outflow = jnp.maximum(speed[d], 0.0) * adjoint_two
        outflow_next = jnp.maximum(speed_next[d], 0.0) * adjoint_pairs[d][0][0]
        change = change + (inflow - inflow_prev) + (outflow_next - outflow)
    adjoint_one = adjoint_two + STEP * change
    force = jnp.stack(
        [STEP * (adjoint_one * grad_first[d] + adjoint_two * grad_second[d]) for d in range(3)]
    )
    hessian = fine_filter(increment) + force
    xlen, ylen, zlen = (hessian.shape[1], hessian.shape[2], hessian.shape[3])
    restricted = jnp.mean(
        hessian.reshape(3, xlen // 4, 4, ylen // 4, 4, zlen // 4, 4), axis=(2, 4, 6)
    )
    coarse = coarse_spread(restricted)
    return expand(coarse) + OMEGA * (hessian - expand(restricted))


def solution(mesh):
    placed = (
        P(None, None, "gy", "gz"),
        P(None, None, "gy", "gz"),
        P(None, "gy", "gz"),
        P(None, "gy", "gz"),
    )
    return jax.shard_map(
        per_device, mesh=mesh, in_specs=placed, out_specs=P(None, None, "gy", "gz"), check_vma=False
    )
```

```python
import functools
import math

import jax
import jax.numpy as jnp
import numpy as np
from jax import lax
from jax.experimental import pallas as pl
from jax.experimental.pallas import tpu as pltpu
from jax.sharding import PartitionSpec as P

MESH = pl.DeviceIdType.MESH
BETA = 0.02
GAMMA = 0.05
COARSE_BETA = 0.025
OMEGA = 1.0 / (0.05 + 42.0 * 0.02)

NX = 256
NR = NX * 8
GY = 32
GZ = 4
CX, CY, CZ = 64, 64, 128
PACK = 32
GROUP = 4
NG = NX // GROUP
HIGH = lax.Precision.HIGHEST


def cas(rows, cols, count):
    angle = (np.outer(rows, cols) % count) * (2.0 * math.pi / count)
    return (np.cos(angle) + np.sin(angle)).astype(np.float32)


def eigen(count):
    return 2.0 - 2.0 * np.cos(np.arange(count) * (2.0 * math.pi / count))


def tables():
    owned = np.concatenate([2 * np.arange(GY), 2 * np.arange(GY) + 1])
    all_x, all_y, all_z = np.arange(CX), np.arange(CY), np.arange(CZ)
    forward_x = cas(owned, all_x, CX)
    inverse_x = cas(all_x, owned, CX)
    forward_y = np.concatenate([cas(all_y, (2 * np.arange(GY) - 1 + j) % CY, CY) for j in range(4)])
    inverse_y = cas(np.concatenate([2 * np.arange(GY), 2 * np.arange(GY) + 1]), all_y, CY)
    both_z = cas(all_z, all_z, CZ)
    gather_z = np.zeros((4 * 128, 128), np.float32)
    spread_z = np.zeros((128, 4 * 128), np.float32)
    for j in range(4):
        for z in range(128):
            gather_z[j * 128 + z, j * 32 + z // 4] = 1.0 / 64.0
            spread_z[j * 32 + z // 4, j * 128 + z] = 1.0
    eigen_yz = (eigen(CY)[:, None] + eigen(CZ)[None, :]).astype(np.float32)
    eigen_x = np.repeat(eigen(CX)[:, None], 128, axis=1).astype(np.float32)
    return (forward_x, inverse_x, forward_y, inverse_y, both_z, gather_z, spread_z, eigen_yz, eigen_x)


def mm(a, b):
    return jnp.dot(a, b, precision=HIGH, preferred_element_type=jnp.float32)


def first(x):
    return pl.multiple_of(x, 8)


def action(
    v_hbm, u_hbm, t_hbm, d_hbm,
    fx, ix, fy, iy, bz, gz_tab, sz, eyz, ex,
    h_hbm, rim_hbm, k_out,
    vel, inc, tb, db, tf, df, s1, a2, w, hs, g0y, g0z, g1y, g1z,
    zsend, zfrom, zpad, wpad, ssend, sfrom, spad, qsend, qfrom, qpad,
    tysend, tyfrom, sysend, syfrom, qysend, qyfrom, rims,
    su, sw, sh, fsend, frecv, bsend, brecv,
    load_sem, zs, zr, ys, yr, rs, rr, fs, fr, bs, br, store_sem,
):
    gz = lax.axis_index("gz")
    gy = lax.axis_index("gy")
    ynext, yprev = lax.rem(gy + 1, GY), lax.rem(gy + GY - 1, GY)
    znext, zprev = lax.rem(gz + 1, GZ), lax.rem(gz + GZ - 1, GZ)
    row = lax.broadcasted_iota(jnp.int32, (8, 128), 0)
    lane = lax.broadcasted_iota(jnp.int32, (8, 128), 1)
    slot = lax.rem(lax.shift_right_logical(lane + 2, 2), PACK)
    low_half = lax.rem(lane + 2, 4) < 2

    barrier = pltpu.get_barrier_semaphore()

    def peer(k):
        return (lax.rem(gz + k // GY, GZ), lax.rem(gy + lax.rem(k, GY), GY))

    def greet(k, carry):
        pl.semaphore_signal(barrier, inc=1, device_id=peer(k), device_id_type=MESH)
        return carry

    loads = [
        pltpu.make_async_copy(src, dst, load_sem.at[i])
        for i, (src, dst) in enumerate(
            [(t_hbm, tb), (d_hbm, db)]
            + [(u_hbm.at[pl.ds(c * NR, NR)], inc.at[pl.ds(c * NR, NR)]) for c in range(3)]
            + [(v_hbm.at[pl.ds(c * NR, NR)], vel.at[pl.ds(c * NR, NR)]) for c in range(3)]
        )
    ]
    for load in loads:
        load.start()
    lax.fori_loop(1, GY * GZ, greet, 0)

    def plane(ref, c, x):
        return ref[pl.ds(first(c * NR + x * 8), 8), :]

    def window(ref, c, i):
        at = [lax.rem(GROUP * i + NX - 1, NX)] + [GROUP * i + q for q in range(GROUP)]
        at.append(lax.rem(GROUP * i + GROUP, NX))
        return [plane(ref, c, x) for x in at]

    def roll(value, shift, axis):
        return pltpu.roll(value, shift % value.shape[axis], axis)

    def pack_into(acc, value, p):
        return jnp.where(slot == p, pltpu.roll(value, 4 * p, 1), acc)

    def unpacked(ref, f, i, q):
        tile = ref[pl.ds(first(f * 64 + (i // 8) * 8), 8), :]
        p = GROUP * lax.rem(i, 8) + q
        return pltpu.roll(tile, lax.rem(128 - 4 * p, 128), 1)

    def z_sides(value, outer):
        up = roll(jnp.where(lane == 0, outer, value), -1, 1)
        down = roll(jnp.where(lane == 127, outer, value), 1, 1)
        return up, down

    def y_sides(value, above, below):
        up = jnp.where(row == 7, above, roll(value, -1, 0))
        down = jnp.where(row == 0, below, roll(value, 1, 0))
        return up, down

    def halo_row(ref, k, x):
        return jnp.broadcast_to(ref[pl.ds(k * NX + x, 1), :], (8, 128))

    def spread(ref, base, k, r):
        return ref[pl.ds(base + 64 * k + r, 8, stride=8), :]

    def z_pair(send, got, sems, base, sem_at):
        size = send.shape[0]
        return [
            pltpu.make_async_remote_copy(
                src_ref=send, dst_ref=got.at[side], send_sem=sems[0].at[sem_at + side],
                recv_sem=sems[1].at[sem_at + side], device_id=(to, gy), device_id_type=MESH)
            for side, to in ((0, znext), (1, zprev))
        ]

    def y_pair(send, got, sems, sem_at):
        return [
            pltpu.make_async_remote_copy(
                src_ref=send.at[side], dst_ref=got.at[side], send_sem=sems[0].at[sem_at + side],
                recv_sem=sems[1].at[sem_at + side], device_id=(gz, to), device_id_type=MESH)
            for side, to in ((0, ynext), (1, yprev))
        ]

    def combine(got, pad, count):
        def one(k, carry):
            at = pl.ds(first(k * 8), 8)
            pad[at, :] = jnp.where(low_half, got[0, at, :], got[1, at, :])
            return carry
        lax.fori_loop(0, count * 8, one, 0)

    loads[0].wait()
    loads[1].wait()

    def widen(k, carry):
        at = pl.ds(pl.multiple_of(k * 64, 64), 64)
        tf[at, :] = tb[at, :].astype(jnp.float32)
        df[at, :] = db[at, :].astype(jnp.float32)
        return carry

    lax.fori_loop(0, NR // 64, widen, 0)

    def state_rows(k, carry):
        at = pl.ds(first(8 * k), 8)
        also = pl.ds(first(NX + 8 * k), 8)
        tysend[0, at, :] = spread(tf, 0, k, 7)
        tysend[0, also, :] = spread(df, 0, k, 7)
        tysend[1, at, :] = spread(tf, 0, k, 0)
        tysend[1, also, :] = spread(df, 0, k, 0)
        return carry

    lax.fori_loop(0, NX // 8, state_rows, 0)
    for c in range(3):
        loads[2 + c].wait()
    sources = [(tf, 0), (df, 0), (inc, 0), (inc, 1), (inc, 2)]

    def pack_inputs(k, carry):
        def some(m, accs):
            for q in range(GROUP):
                p = GROUP * m + q
                accs = tuple(
                    pack_into(acc, plane(ref, c, PACK * k + p), p) for acc, (ref, c) in zip(accs, sources)
                )
            return accs
        accs = lax.fori_loop(0, PACK // GROUP, some, tuple(jnp.zeros((8, 128), jnp.float32) for _ in sources))
        for f, acc in enumerate(accs):
            zsend[pl.ds(first(f * 64 + k * 8), 8), :] = acc
        return carry

    lax.fori_loop(0, NX // PACK, pack_inputs, 0)
    pl.semaphore_wait(barrier, GY * GZ - 1)
    state_copies = y_pair(tysend, tyfrom, (ys, yr), 0)
    edge_copies = z_pair(zsend, zfrom, (zs, zr), 0, 0)
    for copy in edge_copies + state_copies:
        copy.start()

    for copy in edge_copies:
        copy.wait_recv()
    combine(zfrom, zpad, 5)

    def edge_laplacian(n, carry):
        c, k = n // 8, lax.rem(n, 8)
        base = 128 + c * 64

        def tile(ref, m):
            return ref[pl.ds(first(base + m * 8), 8), :]

        here, own = tile(zpad, k), tile(zsend, k)
        before, after = tile(zpad, lax.rem(k + 7, 8)), tile(zpad, lax.rem(k + 1, 8))
        x_down = jnp.where(slot == 0, roll(before, 4, 1), roll(here, 4, 1))
        x_up = jnp.where(slot == PACK - 1, roll(after, -4, 1), roll(here, -4, 1))
        y_up, y_down = y_sides(here, 0.0, 0.0)
        z_sum = jnp.where(low_half, roll(here, 1, 1) + roll(own, -1, 1), roll(here, -1, 1) + roll(own, 1, 1))
        wpad[pl.ds(first(c * 64 + k * 8), 8), :] = 6.0 * here - (x_down + x_up) - (y_up + y_down) - z_sum
        return carry

    lax.fori_loop(0, 24, edge_laplacian, 0)

    def laplacian(i, carry):
        for c in range(3):
            cells = window(inc, c, i)
            sum_u = jnp.zeros((8, 128), jnp.float32)
            sum_w = jnp.zeros((8, 128), jnp.float32)
            for q in range(GROUP):
                u = cells[q + 1]
                z_up, z_down = z_sides(u, unpacked(zpad, 2 + c, i, q))
                y_up, y_down = y_sides(u, 0.0, 0.0)
                lap = 6.0 * u - (cells[q] + cells[q + 2]) - (y_up + y_down) - (z_up + z_down)
                w[pl.ds(first(c * NR + (GROUP * i + q) * 8), 8), :] = lap
                sum_u = sum_u + u
                sum_w = sum_w + lap
            su[pl.ds(first(c * 512 + i * 8), 8), :] = sum_u
            sw[pl.ds(first(c * 512 + i * 8), 8), :] = sum_w
        return carry

    lax.fori_loop(0, NG, laplacian, 0)

    def rim_rows(n, carry):
        c, k = n // 32, lax.rem(n, 32)
        base = c * NR
        at = pl.ds(first(8 * k), 8)
        scale = OMEGA * BETA
        last, first_row = spread(inc, base, k, 7), spread(inc, base, k, 0)
        rims[0, c, 0, at, :] = -scale * (spread(inc, base, k, 6) + 2.0 * spread(w, base, k, 7))
        rims[0, c, 1, at, :] = scale * last
        rims[1, c, 0, at, :] = -scale * (spread(inc, base, k, 1) + 2.0 * spread(w, base, k, 0))
        rims[1, c, 1, at, :] = scale * first_row
        return carry

    lax.fori_loop(0, 96, rim_rows, 0)
    rim_copies = [
        [
            pltpu.make_async_remote_copy(
                src_ref=rims.at[side, c], dst_ref=rim_hbm.at[side, c], send_sem=rs.at[side * 3 + c],
                recv_sem=rr.at[side * 3 + c], device_id=(gz, to), device_id_type=MESH)
            for side, to in ((0, ynext), (1, yprev))
        ]
        for c in range(3)
    ]

    for copy in state_copies:
        copy.wait_recv()

    def differences(ref, field, i, keep_y, keep_z):
        cells = window(ref, 0, i)
        out = []
        for q in range(GROUP):
            x = GROUP * i + q
            z_up, z_down = z_sides(cells[q + 1], unpacked(zpad, field, i, q))
            y_up, y_down = y_sides(
                cells[q + 1], halo_row(tyfrom.at[1], field, x), halo_row(tyfrom.at[0], field, x))
            dy, dz = y_up - y_down, z_up - z_down
            keep_y[pl.ds(first(x * 8), 8), :] = dy
            keep_z[pl.ds(first(x * 8), 8), :] = dz
            out.append((cells[q + 2] - cells[q], dy, dz))
        return out

    def first_state(k, carry):
        def some(m, acc):
            i = 8 * k + m
            for q, (dx, dy, dz) in enumerate(differences(tf, 0, i, g0y, g0z)):
                x = GROUP * i + q
                value = -0.25 * (plane(inc, 0, x) * dx + plane(inc, 1, x) * dy + plane(inc, 2, x) * dz)
                s1[pl.ds(first(x * 8), 8), :] = value
                acc = pack_into(acc, value, GROUP * m + q)
            return acc
        ssend[pl.ds(first(k * 8), 8), :] = lax.fori_loop(0, PACK // GROUP, some, jnp.zeros((8, 128), jnp.float32))
        return carry

    lax.fori_loop(0, NX // PACK, first_state, 0)

    def s1_rows(k, carry):
        at = pl.ds(first(8 * k), 8)
        sysend[0, at, :] = spread(s1, 0, k, 7)
        sysend[1, at, :] = spread(s1, 0, k, 0)
        return carry

    lax.fori_loop(0, NX // 8, s1_rows, 0)
    s1_copies = z_pair(ssend, sfrom, (zs, zr), 0, 2) + y_pair(sysend, syfrom, (ys, yr), 2)
    for copy in s1_copies:
        copy.start()
    for copy in rim_copies[0]:
        copy.start()

    def fine(i, carry):
        for c in range(3):
            cells = window(w, c, i)
            for q in range(GROUP):
                x = GROUP * i + q
                u, lap = plane(inc, c, x), cells[q + 1]
                z_up, z_down = z_sides(lap, unpacked(wpad, c, i, q))
                y_up, y_down = y_sides(lap, -u, -u)
                twice = 6.0 * lap - (cells[q] + cells[q + 2]) - (y_up + y_down) - (z_up + z_down)
                hs[pl.ds(first(c * NR + x * 8), 8), :] = (OMEGA * GAMMA) * u + (OMEGA * BETA) * twice
        return carry

    lax.fori_loop(0, NG, fine, 0)

    for c in range(3):
        loads[5 + c].wait()
    for copy in s1_copies:
        copy.wait_recv()
    combine(sfrom, spad, 1)

    def second_state(k, carry):
        def some(m, acc):
            i = 8 * k + m
            cells = window(s1, 0, i)
            for q, (dx, dy, dz) in enumerate(differences(df, 1, i, g1y, g1z)):
                x = GROUP * i + q
                s = cells[q + 1]
                z_up, z_down = z_sides(s, unpacked(spad, 0, i, q))
                y_up, y_down = y_sides(s, halo_row(syfrom.at[1], 0, x), halo_row(syfrom.at[0], 0, x))
                moved = 0.5 * (plane(inc, 0, x) * dx + plane(inc, 1, x) * dy + plane(inc, 2, x) * dz)
                speed_z = None
                for c, (up, down) in enumerate(((cells[q + 2], cells[q]), (y_up, y_down), (z_up, z_down))):
                    speed = plane(vel, c, x)
                    moved = moved + jnp.maximum(speed, 0.0) * (s - down) + jnp.minimum(speed, 0.0) * (up - s)
                    speed_z = speed
                value = 0.5 * moved - s
                a2[pl.ds(first(x * 8), 8), :] = value
                sent = jnp.where(lane >= 64, jnp.minimum(speed_z, 0.0), jnp.maximum(speed_z, 0.0)) * value
                acc = pack_into(acc, sent, GROUP * m + q)
            return acc
        qsend[pl.ds(first(k * 8), 8), :] = lax.fori_loop(0, PACK // GROUP, some, jnp.zeros((8, 128), jnp.float32))
        return carry

    lax.fori_loop(0, NX // PACK, second_state, 0)

    def flux_rows(k, carry):
        at = pl.ds(first(8 * k), 8)
        qysend[0, at, :] = jnp.minimum(spread(vel, NR, k, 7), 0.0) * spread(a2, 0, k, 7)
        qysend[1, at, :] = jnp.maximum(spread(vel, NR, k, 0), 0.0) * spread(a2, 0, k, 0)
        return carry

    lax.fori_loop(0, NX // 8, flux_rows, 0)
    flux_copies = z_pair(qsend, qfrom, (zs, zr), 0, 4) + y_pair(qysend, qyfrom, (ys, yr), 4)
    for copy in flux_copies:
        copy.start()
    for copy in rim_copies[1]:
        copy.start()
    for copy in flux_copies:
        copy.wait_recv()
    combine(qfrom, qpad, 1)

    def adjoint(i, carry):
        cells_a = window(a2, 0, i)
        cells_v = window(vel, 0, i)
        cells_t = window(tf, 0, i)
        cells_d = window(df, 0, i)
        sums = [jnp.zeros((8, 128), jnp.float32) for _ in range(3)]
        for q in range(GROUP):
            x = GROUP * i + q
            a = cells_a[q + 1]
            vy, vz = plane(vel, 1, x), plane(vel, 2, x)
            size = jnp.abs(cells_v[q + 1]) + jnp.abs(vy) + jnp.abs(vz)
            change = jnp.maximum(cells_v[q + 2], 0.0) * cells_a[q + 2]
            change = change - jnp.minimum(cells_v[q], 0.0) * cells_a[q] - size * a
            qy, py = jnp.minimum(vy, 0.0) * a, jnp.maximum(vy, 0.0) * a
            change = change + jnp.where(row == 7, halo_row(qyfrom.at[1], 0, x), roll(py, -1, 0))
            change = change - jnp.where(row == 0, halo_row(qyfrom.at[0], 0, x), roll(qy, 1, 0))
            qz, pz = jnp.minimum(vz, 0.0) * a, jnp.maximum(vz, 0.0) * a
            outer = unpacked(qpad, 0, i, q)
            change = change + roll(jnp.where(lane == 0, outer, pz), -1, 1)
            change = change - roll(jnp.where(lane == 127, outer, qz), 1, 1)
            scaled = (0.25 * OMEGA) * (a + 0.5 * change)
            other = (0.25 * OMEGA) * a
            pairs = (
                (cells_t[q + 2] - cells_t[q], cells_d[q + 2] - cells_d[q]),
                (plane(g0y, 0, x), plane(g1y, 0, x)),
                (plane(g0z, 0, x), plane(g1z, 0, x)),
            )
            for c, (from_t, from_d) in enumerate(pairs):
                value = plane(hs, c, x) + scaled * from_t + other * from_d
                hs[pl.ds(first(c * NR + x * 8), 8), :] = value
                sums[c] = sums[c] + value
        for c in range(3):
            sh[pl.ds(first(c * 512 + i * 8), 8), :] = sums[c]
        return carry

    lax.fori_loop(0, NG, adjoint, 0)
    store = pltpu.make_async_copy(hs, h_hbm, store_sem)
    store.start()

    def rows_of(ref, c, r):
        return ref[pl.ds(c * 512 + r, CX, stride=8), :]

    parts = []
    for c in range(3):
        scale = OMEGA * BETA
        parts.append(scale * (rows_of(su, c, 0) - rows_of(su, c, 1) - 2.0 * rows_of(sw, c, 0)))
        for half in (0, 4):
            parts.append(
                (rows_of(sh, c, half) + rows_of(sh, c, half + 1))
                + (rows_of(sh, c, half + 2) + rows_of(sh, c, half + 3)))
        parts.append(scale * (rows_of(su, c, 7) - rows_of(su, c, 6) - 2.0 * rows_of(sw, c, 7)))
    for c in range(3):
        lines = mm(fx[...], jnp.concatenate(parts[4 * c:4 * c + 4], axis=1))
        lines = mm(lines, gz_tab[...])
        for h in range(2):
            block = lines[h * GY:(h + 1) * GY]
            if c < 2:
                fsend[h, :, c, :] = block
            else:
                fsend[2 + h, :, 0, :] = block
                fsend[2 + h, :, 1, :] = block

    def exchange(send, got, ssems, rsem):
        def copy_to(k):
            z, y = peer(k)
            return pltpu.make_async_remote_copy(
                src_ref=send.at[z, y], dst_ref=got.at[gz, gy], send_sem=ssems.at[k], recv_sem=rsem,
                device_id=(z, y), device_id_type=MESH)

        def begin(k, carry):
            copy_to(k).start()
            return carry

        def drain(k, carry):
            copy_to(k).wait_send()
            return carry

        lax.fori_loop(1, GY * GZ, begin, 0)
        pltpu.make_async_copy(send.at[gz, gy], got.at[gz, gy], rsem).start()

        def finish():
            pltpu.make_async_copy(got, got, rsem).wait()

        def done():
            lax.fori_loop(1, GY * GZ, drain, 0)

        return finish, done

    arrive, sent_forward = exchange(fsend, frecv, fs, fr)
    for copy in rim_copies[2]:
        copy.start()
    total = eyz[...] + ex[pl.ds(2 * gy + lax.rem(gz, 2), 1), :]
    factor = (1.0 / (GAMMA + COARSE_BETA * total * total) - OMEGA) * (1.0 / (OMEGA * CX * CY * CZ))
    arrive()
    lane64 = lax.broadcasted_iota(jnp.int32, (CY, 128), 1) // 32
    lane32 = lax.broadcasted_iota(jnp.int32, (GY, 128), 1) // 32
    solved = []
    for s in range(2):
        whole = jnp.zeros((CY, 128), jnp.float32)
        for zb in range(GZ):
            lines = mm(fy[...], frecv[zb, :, s, :])
            merged = jnp.zeros((CY, 128), jnp.float32)
            for j in range(4):
                moved = roll(lines[j * CY:(j + 1) * CY], 32 * (zb - j), 1)
                merged = merged + moved
            whole = jnp.where(lane64 == zb, merged, whole)
        modes = mm(whole, bz[...]) * factor
        solved.append(mm(iy[...], mm(modes, bz[...])))
    for zb in range(GZ):
        block = jnp.zeros((GY, 128), jnp.float32)
        for s in range(2):
            for half in range(2):
                part = roll(solved[s][half * GY:(half + 1) * GY], 32 * (2 * s + half - zb), 1)
                block = jnp.where(lane32 == 2 * s + half, part, block)
        bsend[zb, :, 0, :] = block
    arrive, sent_back = exchange(bsend, brecv, bs, br)
    sent_forward()
    arrive()
    for k in range(2):
        modes = jnp.concatenate([brecv[2 * k, :, 0, :], brecv[2 * k + 1, :, 0, :]], axis=0)
        lines = mm(ix[...], modes)
        count = 4 if k == 0 else 2
        wide = mm(lines, sz[:, :count * 128])
        for n in range(count):
            k_out[pl.ds((4 * k + n) * CX, CX), :] = wide[:, n * 128:(n + 1) * 128]

    sent_back()
    for copy in edge_copies + state_copies + s1_copies + flux_copies:
        copy.wait_send()
    for pair in rim_copies:
        for copy in pair:
            copy.wait()
    store.wait()


def finish(h_ref, rim_ref, k_ref, out_ref):
    row = lax.broadcasted_iota(jnp.int32, (8, 128), 0)
    planes = h_ref.shape[1]

    def one(n, carry):
        for q in range(4):
            p = 4 * n + q
            for c in range(3):
                def wide(ref):
                    return jnp.broadcast_to(ref[pl.ds(p, 1), :], (8, 128))

                def coarse(half):
                    return jnp.broadcast_to(k_ref[2 * c + half, pl.ds(n, 1), :], (8, 128))

                rim = jnp.where(row < 4, coarse(0), coarse(1))
                for at, side, kind in ((0, 0, 0), (1, 0, 1), (6, 1, 1), (7, 1, 0)):
                    rim = rim + jnp.where(row == at, wide(rim_ref.at[side, c, kind]), 0.0)
                out_ref[c, p] = h_ref[c, p] + rim
        return carry

    lax.fori_loop(0, planes // 4, one, 0)


def per_device(velocity, increment, template, deformed):
    consts = [jnp.asarray(t) for t in tables()]
    f32 = jnp.float32
    vm = lambda *shape: pltpu.VMEM(shape, f32)
    dma = pltpu.SemaphoreType.DMA
    hessian, rims, coarse = pl.pallas_call(
        action,
        out_shape=(
            jax.ShapeDtypeStruct((3 * NR, 128), f32),
            jax.ShapeDtypeStruct((2, 3, 2, NX, 128), f32),
            jax.ShapeDtypeStruct((6 * CX, 128), f32),
        ),
        in_specs=[pl.BlockSpec(memory_space=pl.ANY)] * 4 + [pl.BlockSpec(memory_space=pltpu.VMEM)] * len(consts),
        out_specs=(
            pl.BlockSpec(memory_space=pl.ANY),
            pl.BlockSpec(memory_space=pl.ANY),
            pl.BlockSpec(memory_space=pltpu.VMEM),
        ),
        scratch_shapes=[
            vm(3 * NR, 128), vm(3 * NR, 128),
            pltpu.VMEM((NR, 128), jnp.bfloat16), pltpu.VMEM((NR, 128), jnp.bfloat16),
            vm(NR, 128), vm(NR, 128), vm(NR, 128), vm(NR, 128), vm(3 * NR, 128), vm(3 * NR, 128),
            vm(NR, 128), vm(NR, 128), vm(NR, 128), vm(NR, 128),
            vm(320, 128), vm(2, 320, 128), vm(320, 128), vm(192, 128),
            vm(64, 128), vm(2, 64, 128), vm(64, 128), vm(64, 128), vm(2, 64, 128), vm(64, 128),
            vm(2, 2 * NX, 128), vm(2, 2 * NX, 128), vm(2, NX, 128), vm(2, NX, 128), vm(2, NX, 128), vm(2, NX, 128),
            vm(2, 3, 2, NX, 128),
            vm(3 * 512, 128), vm(3 * 512, 128), vm(3 * 512, 128),
            vm(GZ, GY, 2, 128), vm(GZ, GY, 2, 128), vm(GZ, GY, 1, 128), vm(GZ, GY, 1, 128),
            dma((8,)), dma((6,)), dma((6,)), dma((6,)), dma((6,)), dma((6,)), dma((6,)),
            dma((GY * GZ,)), dma, dma((GY * GZ,)), dma, dma,
        ],
        compiler_params=pltpu.CompilerParams(
            collective_id=1, has_side_effects=True, vmem_limit_bytes=56 * 1024 * 1024),
        name="action",
    )(
        velocity.reshape(3 * NR, 128), increment.reshape(3 * NR, 128),
        template.reshape(NR, 128), deformed.reshape(NR, 128), *consts,
    )
    step = 32
    return pl.pallas_call(
        finish,
        grid=(NX // step,),
        out_shape=jax.ShapeDtypeStruct((3, NX, 8, 128), f32),
        in_specs=[
            pl.BlockSpec((3, step, 8, 128), lambda i: (0, i, 0, 0)),
            pl.BlockSpec((2, 3, 2, step, 128), lambda i: (0, 0, 0, i, 0)),
            pl.BlockSpec((6, step // 4, 128), lambda i: (0, i, 0)),
        ],
        out_specs=pl.BlockSpec((3, step, 8, 128), lambda i: (0, i, 0, 0)),
        name="finish",
    )(hessian.reshape(3, NX, 8, 128), rims, coarse.reshape(6, CX, 128))


def solution(mesh):
    placed = (
        P(None, None, "gy", "gz"),
        P(None, None, "gy", "gz"),
        P(None, "gy", "gz"),
        P(None, "gy", "gz"),
    )
    return jax.shard_map(
        per_device, mesh=mesh, in_specs=placed, out_specs=P(None, None, "gy", "gz"), check_vma=False
    )
```

```python
import functools
import math

import jax
import jax.numpy as jnp
import numpy as np
from jax import lax
from jax.experimental import pallas as pl
from jax.experimental.pallas import tpu as pltpu
from jax.sharding import PartitionSpec as P

MESH = pl.DeviceIdType.MESH
BETA = 0.02
GAMMA = 0.05
COARSE_BETA = 0.025
OMEGA = 1.0 / (0.05 + 42.0 * 0.02)

NX = 256
NR = NX * 8
GY = 32
GZ = 4
CX, CY, CZ = 64, 64, 128
PACK = 32
GROUP = 4
PAD = 8


def cas(rows, cols, count):
    angle = (np.outer(rows, cols) % count) * (2.0 * math.pi / count)
    return (np.cos(angle) + np.sin(angle)).astype(np.float32)


def eigen(count):
    return 2.0 - 2.0 * np.cos(np.arange(count) * (2.0 * math.pi / count))


def tables():
    owned = np.concatenate([2 * np.arange(GY), 2 * np.arange(GY) + 1])
    all_x, all_y, all_z = np.arange(CX), np.arange(CY), np.arange(CZ)
    forward_x = cas(owned, all_x, CX)
    inverse_x = cas(all_x, owned, CX)
    forward_y = np.concatenate([cas(all_y, (2 * np.arange(GY) - 1 + j) % CY, CY) for j in range(4)])
    inverse_y = cas(np.concatenate([2 * np.arange(GY), 2 * np.arange(GY) + 1]), all_y, CY)
    both_z = cas(all_z, all_z, CZ)
    gather_z = np.zeros((4 * 128, 128), np.float32)
    spread_z = np.zeros((128, 4 * 128), np.float32)
    for j in range(4):
        for z in range(128):
            gather_z[j * 128 + z, j * 32 + z // 4] = 1.0 / 64.0
            spread_z[j * 32 + z // 4, j * 128 + z] = 1.0
    eigen_yz = (eigen(CY)[:, None] + eigen(CZ)[None, :]).astype(np.float32)
    eigen_x = np.repeat(eigen(CX)[:, None], 128, axis=1).astype(np.float32)
    pairs = []
    for table in (forward_x, inverse_x, forward_y, inverse_y, both_z):
        high = table.astype(jnp.bfloat16)
        pairs += [high, (table - high.astype(np.float32)).astype(jnp.bfloat16)]
    return (*pairs, gather_z.astype(jnp.bfloat16), spread_z.astype(jnp.bfloat16), eigen_yz, eigen_x)


TABLES = 14


def halves(value):
    high = value.astype(jnp.bfloat16)
    return high, (value - high.astype(jnp.float32)).astype(jnp.bfloat16)


def mm(a, b):
    (ah, al), (bh, bl) = (x if isinstance(x, tuple) else halves(x) for x in (a, b))
    total = jnp.dot(ah, bh, preferred_element_type=jnp.float32)
    for x, y in ((ah, bl), (al, bh)):
        if x is not None and y is not None:
            total = total + jnp.dot(x, y, preferred_element_type=jnp.float32)
    return total


def first(x):
    return pl.multiple_of(x, 8)


def action(
    v_hbm, u_hbm, t_hbm, d_hbm,
    *refs,
):
    tables_hbm, refs = refs[:TABLES], refs[TABLES:]
    (h_hbm, rim_hbm, k_out), refs = refs[:3], refs[3:]
    tables_vmem, refs = refs[:TABLES], refs[TABLES:]
    fxh, fxl, ixh, ixl, fyh, fyl, iyh, iyl, bzh, bzl, gather, spreader, eyz, ex = tables_vmem
    (
    vel, inc, tb, db, tf, df, s1, a2, w, hs, g0y, g0z, g1y, g1z,
    zsend, zout, zfrom, zpad, wpad, ssend, sout, sfrom, spad, qsend, qout, qfrom, qpad,
    tysend, tyfrom, sysend, syfrom, qysend, qyfrom, rims,
    su, sw, sh, fsend, frecv, bsend, brecv,
    load_sem, zs, zr, ys, yr, rs, rr, fs, fr, bs, br, store_sem,
        table_sem,
    ) = refs
    gz = lax.axis_index("gz")
    gy = lax.axis_index("gy")
    ynext, yprev = lax.rem(gy + 1, GY), lax.rem(gy + GY - 1, GY)
    znext, zprev = lax.rem(gz + 1, GZ), lax.rem(gz + GZ - 1, GZ)
    row = lax.broadcasted_iota(jnp.int32, (8, 128), 0)
    lane = lax.broadcasted_iota(jnp.int32, (8, 128), 1)
    slot = lax.rem(lax.shift_right_logical(lane + 2, 2), PACK)
    low_half = lax.rem(lane + 2, 4) < 2

    barrier = pltpu.get_barrier_semaphore()
    packs = NX // PACK

    def wrapped(k, count):
        return lax.select(k >= count, k - count, k)

    def each_peer(act):
        for kz in range(GZ):
            z = wrapped(gz + kz, GZ)

            def one(ky, carry):
                act(kz * GY + ky, z, wrapped(gy + ky, GY))
                return carry

            if kz == 0:
                for ky in range(1, 8):
                    one(ky, 0)
            lax.fori_loop(0 if kz else 8, GY, one, 0, unroll=8)

    def greet(k, z, y):
        pl.semaphore_signal(barrier, inc=1, device_id=(z, y), device_id_type=MESH)

    loads = [
        pltpu.make_async_copy(src, dst, load_sem.at[i])
        for i, (src, dst) in enumerate(
            [(t_hbm, tb), (d_hbm, db)]
            + [(u_hbm.at[pl.ds(c * NR, NR)], inc.at[pl.ds(PAD + c * NR, NR)]) for c in range(3)]
            + [(v_hbm.at[pl.ds(c * NR, NR)], vel.at[pl.ds(PAD + c * NR, NR)]) for c in range(3)]
        )
    ]
    fetches = [
        pltpu.make_async_copy(src, dst, table_sem.at[i]) for i, (src, dst) in enumerate(zip(tables_hbm, tables_vmem))
    ]
    for load in loads[:5]:
        load.start()
    each_peer(greet)

    def plane(ref, c, x):
        return ref[pl.ds(first(PAD + c * NR + x * 8), 8), :]

    def put(ref, c, x, value):
        ref[pl.ds(first(PAD + c * NR + x * 8), 8), :] = value

    def y_up(ref, c, x):
        return ref[pl.ds(PAD + 1 + c * NR + x * 8, 8), :]

    def y_down(ref, c, x):
        return ref[pl.ds(PAD - 1 + c * NR + x * 8, 8), :]

    def walk(ref, c, k):
        before = plane(ref, c, lax.rem(PACK * k + NX - 1, NX))
        here = plane(ref, c, PACK * k)
        for p in range(PACK):
            x = PACK * k + p + 1
            after = plane(ref, c, x if p < PACK - 1 else lax.rem(x, NX))
            yield before, here, after
            before, here = here, after

    def roll(value, shift, axis):
        return pltpu.roll(value, shift % value.shape[axis], axis)

    def pack_into(acc, value, p):
        return jnp.where(slot == p, roll(value, 4 * p, 1), acc)

    def unpacked(ref, f, k, p):
        return roll(ref[pl.ds(first(f * 64 + k * 8), 8), :], -4 * p, 1)

    def z_sides(value, outer):
        up = roll(jnp.where(lane == 0, outer, value), -1, 1)
        down = roll(jnp.where(lane == 127, outer, value), 1, 1)
        return up, down

    def halo_row(ref, k, x):
        return jnp.broadcast_to(ref[pl.ds(k * NX + x, 1), :], (8, 128))

    def spread(ref, base, k, r):
        return ref[pl.ds(PAD + base + 64 * k + r, 8, stride=8), :]

    def fold(packed, send, count):
        def one(m, carry):
            even = packed[pl.ds(first(m * 16), 8), :]
            odd = packed[pl.ds(first(m * 16 + 8), 8), :]
            at = pl.ds(first(m * 8), 8)
            send[0, at, :] = jnp.where(low_half, even, roll(odd, 2, 1))
            send[1, at, :] = jnp.where(low_half, roll(odd, -2, 1), even)
            return carry
        lax.fori_loop(0, count * 4, one, 0)

    def z_pair(send, got, sems, sem_at):
        return [
            pltpu.make_async_remote_copy(
                src_ref=send.at[side], dst_ref=got.at[side], send_sem=sems[0].at[sem_at + side],
                recv_sem=sems[1].at[sem_at + side], device_id=(to, gy), device_id_type=MESH)
            for side, to in ((0, znext), (1, zprev))
        ]

    def y_pair(send, got, sems, sem_at):
        return [
            pltpu.make_async_remote_copy(
                src_ref=send.at[side], dst_ref=got.at[side], send_sem=sems[0].at[sem_at + side],
                recv_sem=sems[1].at[sem_at + side], device_id=(gz, to), device_id_type=MESH)
            for side, to in ((0, ynext), (1, yprev))
        ]

    def combine(got, pad, count):
        def one(m, carry):
            at = pl.ds(first(m * 8), 8)
            below, above = got[0, at, :], got[1, at, :]
            pad[pl.ds(first(m * 16), 8), :] = jnp.where(low_half, below, above)
            pad[pl.ds(first(m * 16 + 8), 8), :] = jnp.where(low_half, roll(below, -2, 1), roll(above, 2, 1))
            return carry
        lax.fori_loop(0, count * 4, one, 0)

    loads[0].wait()
    loads[1].wait()

    def widen(k, carry):
        at = pl.ds(pl.multiple_of(k * 64, 64), 64)
        to = pl.ds(first(PAD + k * 64), 64)
        tf[to, :] = tb[at, :].astype(jnp.float32)
        df[to, :] = db[at, :].astype(jnp.float32)
        return carry

    lax.fori_loop(0, NR // 64, widen, 0)

    def state_rows(k, carry):
        at = pl.ds(first(8 * k), 8)
        also = pl.ds(first(NX + 8 * k), 8)
        tysend[0, at, :] = spread(tf, 0, k, 7)
        tysend[0, also, :] = spread(df, 0, k, 7)
        tysend[1, at, :] = spread(tf, 0, k, 0)
        tysend[1, also, :] = spread(df, 0, k, 0)
        return carry

    lax.fori_loop(0, NX // 8, state_rows, 0)
    for c in range(3):
        loads[2 + c].wait()
    for load in loads[5:] + fetches:
        load.start()
    sources = [(tf, 0), (df, 0), (inc, 0), (inc, 1), (inc, 2)]

    def inner_rows(n, carry):
        c, k = n // 32, lax.rem(n, 32)
        at = pl.ds(first(8 * k), 8)
        rims[0, c, 1, at, :] = spread(inc, c * NR, k, 7)
        rims[1, c, 1, at, :] = spread(inc, c * NR, k, 0)
        return carry

    def outer_rows(n, carry):
        c, k = n // 32, lax.rem(n, 32)
        at = pl.ds(first(8 * k), 8)
        rims[0, c, 0, at, :] = -(spread(inc, c * NR, k, 6) + 2.0 * spread(w, c * NR, k, 7))
        rims[1, c, 0, at, :] = -(spread(inc, c * NR, k, 1) + 2.0 * spread(w, c * NR, k, 0))
        return carry

    rim_copies = {
        (c, kind): [
            pltpu.make_async_remote_copy(
                src_ref=rims.at[side, c, kind], dst_ref=rim_hbm.at[side, c, kind],
                send_sem=rs.at[side * 6 + c * 2 + kind], recv_sem=rr.at[side * 6 + c * 2 + kind],
                device_id=(gz, to), device_id_type=MESH)
            for side, to in ((0, ynext), (1, yprev))
        ]
        for c in range(3) for kind in range(2)
    }

    def begin_rims(*which):
        for one in which:
            for copy in rim_copies[one]:
                copy.start()

    lax.fori_loop(0, 96, inner_rows, 0)

    def pack_inputs(k, carry):
        for f, (ref, c) in enumerate(sources):
            acc = jnp.zeros((8, 128), jnp.float32)
            for p in range(PACK):
                acc = pack_into(acc, plane(ref, c, PACK * k + p), p)
            zsend[pl.ds(first(f * 64 + k * 8), 8), :] = acc
        return carry

    lax.fori_loop(0, packs, pack_inputs, 0)
    fold(zsend, zout, 5)
    pl.semaphore_wait(barrier, GY * GZ - 1)
    state_copies = y_pair(tysend, tyfrom, (ys, yr), 0)
    edge_copies = z_pair(zout, zfrom, (zs, zr), 0)
    for copy in edge_copies + state_copies:
        copy.start()

    for copy in edge_copies:
        copy.wait_recv()
    combine(zfrom, zpad, 5)

    def edge_laplacian(n, carry):
        c, k = n // 8, lax.rem(n, 8)
        base = 128 + c * 64

        def tile(ref, m):
            return ref[pl.ds(first(base + m * 8), 8), :]

        here, own = tile(zpad, k), tile(zsend, k)
        before, after = tile(zpad, lax.rem(k + 7, 8)), tile(zpad, lax.rem(k + 1, 8))
        x_down = jnp.where(slot == 0, roll(before, 4, 1), roll(here, 4, 1))
        x_up = jnp.where(slot == PACK - 1, roll(after, -4, 1), roll(here, -4, 1))
        y_sum = jnp.where(row == 7, 0.0, roll(here, -1, 0)) + jnp.where(row == 0, 0.0, roll(here, 1, 0))
        z_sum = jnp.where(low_half, roll(here, 1, 1) + roll(own, -1, 1), roll(here, -1, 1) + roll(own, 1, 1))
        wpad[pl.ds(first(c * 64 + k * 8), 8), :] = 6.0 * here - (x_down + x_up) - y_sum - z_sum
        return carry

    lax.fori_loop(0, 24, edge_laplacian, 0)

    def y_sum_closed(ref, c, x, beyond):
        return jnp.where(row == 7, beyond, y_up(ref, c, x)) + jnp.where(row == 0, beyond, y_down(ref, c, x))

    def laplacian(n, carry):
        c, k = n // packs, lax.rem(n, packs)
        cells = walk(inc, c, k)
        for i in range(PACK // GROUP):
            sum_u = jnp.zeros((8, 128), jnp.float32)
            sum_w = jnp.zeros((8, 128), jnp.float32)
            for p in range(GROUP * i, GROUP * i + GROUP):
                x = PACK * k + p
                before, u, after = next(cells)
                up, down = z_sides(u, unpacked(zpad, 2 + c, k, p))
                lap = 6.0 * u - (before + after) - y_sum_closed(inc, c, x, 0.0) - (up + down)
                put(w, c, x, lap)
                sum_u = sum_u + u
                sum_w = sum_w + lap
            at = pl.ds(first(c * 512 + k * 64 + i * 8), 8)
            su[at, :] = sum_u
            sw[at, :] = sum_w
        return carry

    lax.fori_loop(0, packs, laplacian, 0)

    for copy in state_copies:
        copy.wait_recv()

    begin_rims((0, 1))

    def differences(ref, field, k, keep_y, keep_z):
        for p, (before, here, after) in enumerate(walk(ref, 0, k)):
            x = PACK * k + p
            z_up, z_down = z_sides(here, unpacked(zpad, field, k, p))
            up = jnp.where(row == 7, halo_row(tyfrom.at[1], field, x), y_up(ref, 0, x))
            down = jnp.where(row == 0, halo_row(tyfrom.at[0], field, x), y_down(ref, 0, x))
            dy, dz = up - down, z_up - z_down
            put(keep_y, 0, x, dy)
            put(keep_z, 0, x, dz)
            yield after - before, dy, dz

    def first_state(k, carry):
        acc = jnp.zeros((8, 128), jnp.float32)
        for p, (dx, dy, dz) in enumerate(differences(tf, 0, k, g0y, g0z)):
            x = PACK * k + p
            value = -0.25 * (plane(inc, 0, x) * dx + plane(inc, 1, x) * dy + plane(inc, 2, x) * dz)
            put(s1, 0, x, value)
            acc = pack_into(acc, value, p)
        ssend[pl.ds(first(k * 8), 8), :] = acc
        return carry

    lax.fori_loop(0, packs, first_state, 0)
    fold(ssend, sout, 1)

    def s1_rows(k, carry):
        at = pl.ds(first(8 * k), 8)
        sysend[0, at, :] = spread(s1, 0, k, 7)
        sysend[1, at, :] = spread(s1, 0, k, 0)
        return carry

    lax.fori_loop(0, NX // 8, s1_rows, 0)
    s1_copies = z_pair(sout, sfrom, (zs, zr), 2) + y_pair(sysend, syfrom, (ys, yr), 2)
    for copy in s1_copies:
        copy.start()


    def fine(n, carry):
        c, k = n // packs, lax.rem(n, packs)
        for p, (before, lap, after) in enumerate(walk(w, c, k)):
            x = PACK * k + p
            u = plane(inc, c, x)
            up, down = z_sides(lap, unpacked(wpad, c, k, p))
            twice = 6.0 * lap - (before + after) - y_sum_closed(w, c, x, -u) - (up + down)
            put(hs, c, x, (OMEGA * GAMMA) * u + (OMEGA * BETA) * twice)
        return carry

    lax.fori_loop(packs, 3 * packs, laplacian, 0)
    lax.fori_loop(0, packs, fine, 0)

    for c in range(3):
        loads[5 + c].wait()
    for copy in s1_copies:
        copy.wait_recv()
    begin_rims((1, 1), (2, 1))
    combine(sfrom, spad, 1)

    def second_state(k, carry):
        acc = jnp.zeros((8, 128), jnp.float32)
        both = zip(differences(df, 1, k, g1y, g1z), walk(s1, 0, k))
        for p, ((dx, dy, dz), (s_before, s, s_after)) in enumerate(both):
            x = PACK * k + p
            z_up, z_down = z_sides(s, unpacked(spad, 0, k, p))
            up = jnp.where(row == 7, halo_row(syfrom.at[1], 0, x), y_up(s1, 0, x))
            down = jnp.where(row == 0, halo_row(syfrom.at[0], 0, x), y_down(s1, 0, x))
            moved = 0.5 * (plane(inc, 0, x) * dx + plane(inc, 1, x) * dy + plane(inc, 2, x) * dz)
            speed = None
            for c, (after, before) in enumerate(((s_after, s_before), (up, down), (z_up, z_down))):
                speed = plane(vel, c, x)
                moved = moved + jnp.maximum(speed, 0.0) * (s - before) + jnp.minimum(speed, 0.0) * (after - s)
            value = 0.5 * moved - s
            put(a2, 0, x, value)
            sent = jnp.where(lane >= 64, jnp.minimum(speed, 0.0), jnp.maximum(speed, 0.0)) * value
            acc = pack_into(acc, sent, p)
        qsend[pl.ds(first(k * 8), 8), :] = acc
        return carry

    lax.fori_loop(0, packs, second_state, 0)
    fold(qsend, qout, 1)

    def flux_rows(k, carry):
        at = pl.ds(first(8 * k), 8)
        qysend[0, at, :] = jnp.minimum(spread(vel, NR, k, 7), 0.0) * spread(a2, 0, k, 7)
        qysend[1, at, :] = jnp.maximum(spread(vel, NR, k, 0), 0.0) * spread(a2, 0, k, 0)
        return carry

    lax.fori_loop(0, NX // 8, flux_rows, 0)
    flux_copies = z_pair(qout, qfrom, (zs, zr), 4) + y_pair(qysend, qyfrom, (ys, yr), 4)
    for copy in flux_copies:
        copy.start()
    lax.fori_loop(0, 96, outer_rows, 0)
    lax.fori_loop(packs, 3 * packs, fine, 0)
    for copy in flux_copies:
        copy.wait_recv()
    begin_rims((0, 0))
    combine(qfrom, qpad, 1)

    def adjoint(k, carry):
        sums = []
        fields = zip(walk(a2, 0, k), walk(vel, 0, k), walk(tf, 0, k), walk(df, 0, k))
        for p, (near_a, near_v, near_t, near_d) in enumerate(fields):
            x = PACK * k + p
            if p % GROUP == 0:
                sums = [jnp.zeros((8, 128), jnp.float32) for _ in range(3)]
            a = near_a[1]
            vy, vz = plane(vel, 1, x), plane(vel, 2, x)
            size = jnp.abs(near_v[1]) + jnp.abs(vy) + jnp.abs(vz)
            change = jnp.maximum(near_v[2], 0.0) * near_a[2]
            change = change - jnp.minimum(near_v[0], 0.0) * near_a[0] - size * a
            p_up = jnp.maximum(y_up(vel, 1, x), 0.0) * y_up(a2, 0, x)
            q_down = jnp.minimum(y_down(vel, 1, x), 0.0) * y_down(a2, 0, x)
            change = change + jnp.where(row == 7, halo_row(qyfrom.at[1], 0, x), p_up)
            change = change - jnp.where(row == 0, halo_row(qyfrom.at[0], 0, x), q_down)
            qz, pz = jnp.minimum(vz, 0.0) * a, jnp.maximum(vz, 0.0) * a
            outer = unpacked(qpad, 0, k, p)
            change = change + roll(jnp.where(lane == 0, outer, pz), -1, 1)
            change = change - roll(jnp.where(lane == 127, outer, qz), 1, 1)
            scaled = (0.25 * OMEGA) * (a + 0.5 * change)
            other = (0.25 * OMEGA) * a
            pairs = (
                (near_t[2] - near_t[0], near_d[2] - near_d[0]),
                (plane(g0y, 0, x), plane(g1y, 0, x)),
                (plane(g0z, 0, x), plane(g1z, 0, x)),
            )
            for c, (from_t, from_d) in enumerate(pairs):
                value = plane(hs, c, x) + scaled * from_t + other * from_d
                put(hs, c, x, value)
                sums[c] = sums[c] + value
            if p % GROUP == GROUP - 1:
                for c in range(3):
                    sh[pl.ds(first(c * 512 + k * 64 + p // GROUP * 8), 8), :] = sums[c]
        return carry

    lax.fori_loop(0, packs, adjoint, 0)
    store = pltpu.make_async_copy(hs.at[pl.ds(PAD, 3 * NR)], h_hbm, store_sem)
    store.start()

    def rows_of(ref, c, r):
        return ref[pl.ds(c * 512 + r, CX, stride=8), :]

    for fetch in fetches:
        fetch.wait()

    def contribute():
        parts = []
        for c in range(3):
            scale = OMEGA * BETA
            parts.append(scale * (rows_of(su, c, 0) - rows_of(su, c, 1) - 2.0 * rows_of(sw, c, 0)))
            for half in (0, 4):
                parts.append(
                    (rows_of(sh, c, half) + rows_of(sh, c, half + 1))
                    + (rows_of(sh, c, half + 2) + rows_of(sh, c, half + 3)))
            parts.append(scale * (rows_of(su, c, 7) - rows_of(su, c, 6) - 2.0 * rows_of(sw, c, 7)))
        for c in range(3):
            lines = mm((fxh[...], fxl[...]), jnp.concatenate(parts[4 * c:4 * c + 4], axis=1))
            lines = mm(lines, (gather[...], None))
            for h in range(2):
                block = lines[h * GY:(h + 1) * GY]
                if c < 2:
                    fsend[h * GY:(h + 1) * GY, c, :] = block
                else:
                    fsend[(2 + h) * GY:(3 + h) * GY, 0, :] = block
                    fsend[(2 + h) * GY:(3 + h) * GY, 1, :] = block

    contribute()
    me = gz * GY + gy

    def exchange(send, got, ssem, rsem):
        def begin(k, z, y):
            pltpu.make_async_remote_copy(
                src_ref=send.at[z * GY + y], dst_ref=got.at[me], send_sem=ssem, recv_sem=rsem,
                device_id=(z, y), device_id_type=MESH).start()

        each_peer(begin)
        pltpu.make_async_copy(send.at[me], got.at[me], rsem).start()

        def finish():
            pltpu.make_async_copy(got, got, rsem).wait()

        def done():
            others = pl.ds(0, GY * GZ - 1)
            pltpu.make_async_copy(send.at[others], send.at[others], ssem).wait()

        return finish, done

    arrive, sent_forward = exchange(fsend, frecv, fs, fr)
    begin_rims((1, 0), (2, 0))
    total = eyz[...] + ex[pl.ds(2 * gy + lax.rem(gz, 2), 1), :]
    factor = (1.0 / (GAMMA + COARSE_BETA * total * total) - OMEGA) * (1.0 / (OMEGA * CX * CY * CZ))
    arrive()
    lane64 = lax.broadcasted_iota(jnp.int32, (CY, 128), 1) // 32
    lane32 = lax.broadcasted_iota(jnp.int32, (GY, 128), 1) // 32
    def solve():
        solved = []
        for s in range(2):
            whole = jnp.zeros((CY, 128), jnp.float32)
            for zb in range(GZ):
                lines = mm((fyh[...], fyl[...]), frecv[zb * GY:(zb + 1) * GY, s, :])
                merged = jnp.zeros((CY, 128), jnp.float32)
                for j in range(4):
                    moved = roll(lines[j * CY:(j + 1) * CY], 32 * (zb - j), 1)
                    merged = merged + moved
                whole = jnp.where(lane64 == zb, merged, whole)
            table_z = (bzh[...], bzl[...])
            modes = mm(whole, table_z) * factor
            solved.append(mm((iyh[...], iyl[...]), mm(modes, table_z)))
        for zb in range(GZ):
            block = jnp.zeros((GY, 128), jnp.float32)
            for s in range(2):
                for half in range(2):
                    part = roll(solved[s][half * GY:(half + 1) * GY], 32 * (2 * s + half - zb), 1)
                    block = jnp.where(lane32 == 2 * s + half, part, block)
            bsend[zb * GY:(zb + 1) * GY, 0, :] = block

    solve()
    arrive, sent_back = exchange(bsend, brecv, bs, br)
    arrive()
    def bring_back():
        for k in range(2):
            modes = brecv[2 * k * GY:(2 * k + 2) * GY, 0, :]
            lines = mm((ixh[...], ixl[...]), modes)
            count = 4 if k == 0 else 2
            wide = mm(lines, (spreader[:, :count * 128], None))
            for n in range(count):
                k_out[pl.ds((4 * k + n) * CX, CX), :] = wide[:, n * 128:(n + 1) * 128]

    bring_back()
    sent_forward()
    sent_back()
    for copy in edge_copies + state_copies + s1_copies + flux_copies:
        copy.wait_send()
    for pair in rim_copies.values():
        for copy in pair:
            copy.wait()
    store.wait()


def finish(h_ref, rim_ref, k_ref, out_ref):
    row = lax.broadcasted_iota(jnp.int32, (8, 128), 0)

    def one(c, carry):
        for p in range(h_ref.shape[1]):
            def wide(ref):
                return jnp.broadcast_to(ref[pl.ds(p, 1), :], (8, 128))

            rim = jnp.where(
                row < 4, *(jnp.broadcast_to(k_ref[2 * c + half, pl.ds(p // 4, 1), :], (8, 128)) for half in (0, 1)))
            late = jnp.zeros((8, 128), jnp.float32)
            for at, side, kind in ((0, 0, 0), (1, 0, 1), (6, 1, 1), (7, 1, 0)):
                late = jnp.where(row == at, wide(rim_ref.at[side, c, kind]), late)
            out_ref[c, p] = h_ref[c, p] + (rim + (OMEGA * BETA) * late)
        return carry

    lax.fori_loop(0, 3, one, 0)


def per_device(velocity, increment, template, deformed):
    consts = [jnp.asarray(t) for t in tables()]
    f32 = jnp.float32
    vm = lambda *shape: pltpu.VMEM(shape, f32)
    dma = pltpu.SemaphoreType.DMA
    hessian, rims, coarse = pl.pallas_call(
        action,
        out_shape=(
            jax.ShapeDtypeStruct((3 * NR, 128), f32),
            jax.ShapeDtypeStruct((2, 3, 2, NX, 128), f32),
            jax.ShapeDtypeStruct((6 * CX, 128), f32),
        ),
        in_specs=[pl.BlockSpec(memory_space=pl.ANY)] * (4 + len(consts)),
        out_specs=(
            pl.BlockSpec(memory_space=pl.ANY),
            pl.BlockSpec(memory_space=pl.ANY),
            pl.BlockSpec(memory_space=pltpu.VMEM),
        ),
        scratch_shapes=[
            *[pltpu.VMEM(t.shape, t.dtype) for t in consts],
            vm(3 * NR + 2 * PAD, 128), vm(3 * NR + 2 * PAD, 128),
            pltpu.VMEM((NR, 128), jnp.bfloat16), pltpu.VMEM((NR, 128), jnp.bfloat16),
            *[vm(NR + 2 * PAD, 128)] * 4, *[vm(3 * NR + 2 * PAD, 128)] * 2, *[vm(NR + 2 * PAD, 128)] * 4,
            vm(320, 128), vm(2, 160, 128), vm(2, 160, 128), vm(320, 128), vm(192, 128),
            *[vm(64, 128), vm(2, 32, 128), vm(2, 32, 128), vm(64, 128)] * 2,
            vm(2, 2 * NX, 128), vm(2, 2 * NX, 128), vm(2, NX, 128), vm(2, NX, 128), vm(2, NX, 128), vm(2, NX, 128),
            vm(2, 3, 2, NX, 128),
            vm(3 * 512, 128), vm(3 * 512, 128), vm(3 * 512, 128),
            vm(GZ * GY, 2, 128), vm(GZ * GY, 2, 128), vm(GZ * GY, 1, 128), vm(GZ * GY, 1, 128),
            dma((8,)), dma((6,)), dma((6,)), dma((6,)), dma((6,)), dma((12,)), dma((12,)),
            dma, dma, dma, dma, dma, dma((TABLES,)),
        ],
        compiler_params=pltpu.CompilerParams(
            collective_id=1, has_side_effects=True, vmem_limit_bytes=56 * 1024 * 1024),
        name="action",
    )(
        velocity.reshape(3 * NR, 128), increment.reshape(3 * NR, 128),
        template.reshape(NR, 128), deformed.reshape(NR, 128), *consts,
    )
    step = 32
    return pl.pallas_call(
        finish,
        grid=(NX // step,),
        out_shape=jax.ShapeDtypeStruct((3, NX, 8, 128), f32),
        in_specs=[
            pl.BlockSpec((3, step, 8, 128), lambda i: (0, i, 0, 0)),
            pl.BlockSpec((2, 3, 2, step, 128), lambda i: (0, 0, 0, i, 0)),
            pl.BlockSpec((6, step // 4, 128), lambda i: (0, i, 0)),
        ],
        out_specs=pl.BlockSpec((3, step, 8, 128), lambda i: (0, i, 0, 0)),
        name="finish",
    )(hessian.reshape(3, NX, 8, 128), rims, coarse.reshape(6, CX, 128))


def solution(mesh):
    placed = (
        P(None, None, "gy", "gz"),
        P(None, None, "gy", "gz"),
        P(None, "gy", "gz"),
        P(None, "gy", "gz"),
    )
    return jax.shard_map(
        per_device, mesh=mesh, in_specs=placed, out_specs=P(None, None, "gy", "gz"), check_vma=False
    )
```

```python
import functools
import math

import jax
import jax.numpy as jnp
import numpy as np
from jax import lax
from jax.experimental import pallas as pl
from jax.experimental.pallas import tpu as pltpu
from jax.sharding import PartitionSpec as P

MESH = pl.DeviceIdType.MESH
BETA = 0.02
GAMMA = 0.05
COARSE_BETA = 0.025
OMEGA = 1.0 / (0.05 + 42.0 * 0.02)

NX = 256
NR = NX * 8
GY = 32
GZ = 4
CX, CY, CZ = 64, 64, 128
PACK = 32
GROUP = 4
PAD = 8


def cas(rows, cols, count):
    angle = (np.outer(rows, cols) % count) * (2.0 * math.pi / count)
    return (np.cos(angle) + np.sin(angle)).astype(np.float32)


def eigen(count):
    return 2.0 - 2.0 * np.cos(np.arange(count) * (2.0 * math.pi / count))


def tables():
    owned = np.concatenate([2 * np.arange(GY), 2 * np.arange(GY) + 1])
    all_x, all_y, all_z = np.arange(CX), np.arange(CY), np.arange(CZ)
    forward_x = cas(owned, all_x, CX)
    inverse_x = cas(all_x, owned, CX)
    forward_y = np.concatenate([cas(all_y, (2 * np.arange(GY) - 1 + j) % CY, CY) for j in range(4)])
    inverse_y = cas(np.concatenate([2 * np.arange(GY), 2 * np.arange(GY) + 1]), all_y, CY)
    both_z = cas(all_z, all_z, CZ)
    gather_z = np.zeros((4 * 128, 128), np.float32)
    spread_z = np.zeros((128, 4 * 128), np.float32)
    for j in range(4):
        for z in range(128):
            gather_z[j * 128 + z, j * 32 + z // 4] = 1.0 / 64.0
            spread_z[j * 32 + z // 4, j * 128 + z] = 1.0
    eigen_yz = (eigen(CY)[:, None] + eigen(CZ)[None, :]).astype(np.float32)
    eigen_x = np.repeat(eigen(CX)[:, None], 128, axis=1).astype(np.float32)
    pairs = []
    for table in (forward_x, inverse_x, forward_y, inverse_y, both_z):
        high = table.astype(jnp.bfloat16)
        pairs += [high, (table - high.astype(np.float32)).astype(jnp.bfloat16)]
    return (*pairs, gather_z.astype(jnp.bfloat16), spread_z.astype(jnp.bfloat16), eigen_yz, eigen_x)


TABLES = 14


def halves(value):
    high = value.astype(jnp.bfloat16)
    return high, (value - high.astype(jnp.float32)).astype(jnp.bfloat16)


def mm(a, b):
    (ah, al), (bh, bl) = (x if isinstance(x, tuple) else halves(x) for x in (a, b))
    total = jnp.dot(ah, bh, preferred_element_type=jnp.float32)
    for x, y in ((ah, bl), (al, bh)):
        if x is not None and y is not None:
            total = total + jnp.dot(x, y, preferred_element_type=jnp.float32)
    return total


def first(x):
    return pl.multiple_of(x, 8)


def action(
    v_hbm, u_hbm, t_hbm, d_hbm,
    *refs,
):
    tables_hbm, refs = refs[:TABLES], refs[TABLES:]
    (hs, rim_in, k_out), refs = refs[:3], refs[3:]
    tables_vmem, refs = refs[:TABLES], refs[TABLES:]
    fxh, fxl, ixh, ixl, fyh, fyl, iyh, iyl, bzh, bzl, gather, spreader, eyz, ex = tables_vmem
    (
    vel, inc, tb, db, tf, df, s1, a2, w, g0y, g0z, g1y, g1z,
    zsend, zout, zfrom, zpad, wpad, ssend, sout, sfrom, spad, qsend, qout, qfrom, qpad,
    tysend, tyfrom, sysend, syfrom, qysend, qyfrom, rims,
    su, sw, sh, fsend, frecv, bsend, brecv,
    load_sem, zs, zr, ys, yr, rs, rr, fs, fr, bs, br,
        table_sem,
    ) = refs
    gz = lax.axis_index("gz")
    gy = lax.axis_index("gy")
    ynext, yprev = lax.rem(gy + 1, GY), lax.rem(gy + GY - 1, GY)
    znext, zprev = lax.rem(gz + 1, GZ), lax.rem(gz + GZ - 1, GZ)
    row = lax.broadcasted_iota(jnp.int32, (8, 128), 0)
    lane = lax.broadcasted_iota(jnp.int32, (8, 128), 1)
    slot = lax.rem(lax.shift_right_logical(lane + 2, 2), PACK)
    low_half = lax.rem(lane + 2, 4) < 2

    barrier = pltpu.get_barrier_semaphore()
    packs = NX // PACK

    def wrapped(k, count):
        return lax.select(k >= count, k - count, k)

    def each_peer(act):
        for kz in range(GZ):
            z = wrapped(gz + kz, GZ)

            def one(ky, carry):
                act(kz * GY + ky, z, wrapped(gy + ky, GY))
                return carry

            if kz == 0:
                for ky in range(1, 8):
                    one(ky, 0)
            lax.fori_loop(0 if kz else 8, GY, one, 0, unroll=8)

    def greet(k, z, y):
        pl.semaphore_signal(barrier, inc=1, device_id=(z, y), device_id_type=MESH)

    loads = [
        pltpu.make_async_copy(src, dst, load_sem.at[i])
        for i, (src, dst) in enumerate(
            [(t_hbm, tb), (d_hbm, db)]
            + [(u_hbm.at[pl.ds(c * NR, NR)], inc.at[pl.ds(PAD + c * NR, NR)]) for c in range(3)]
            + [(v_hbm.at[pl.ds(c * NR, NR)], vel.at[pl.ds(PAD + c * NR, NR)]) for c in range(3)]
        )
    ]
    fetches = [
        pltpu.make_async_copy(src, dst, table_sem.at[i]) for i, (src, dst) in enumerate(zip(tables_hbm, tables_vmem))
    ]
    for load in loads[:5]:
        load.start()
    each_peer(greet)

    def plane(ref, c, x):
        return ref[pl.ds(first(PAD + c * NR + x * 8), 8), :]

    def put(ref, c, x, value):
        ref[pl.ds(first(PAD + c * NR + x * 8), 8), :] = value

    def y_up(ref, c, x):
        return ref[pl.ds(PAD + 1 + c * NR + x * 8, 8), :]

    def y_down(ref, c, x):
        return ref[pl.ds(PAD - 1 + c * NR + x * 8, 8), :]

    def walk(ref, c, k):
        before = plane(ref, c, lax.rem(PACK * k + NX - 1, NX))
        here = plane(ref, c, PACK * k)
        for p in range(PACK):
            x = PACK * k + p + 1
            after = plane(ref, c, x if p < PACK - 1 else lax.rem(x, NX))
            yield before, here, after
            before, here = here, after

    def roll(value, shift, axis):
        return pltpu.roll(value, shift % value.shape[axis], axis)

    def pack_into(acc, value, p):
        return jnp.where(slot == p, roll(value, 4 * p, 1), acc)

    def unpacked(ref, f, k, p):
        return roll(ref[pl.ds(first(f * 64 + k * 8), 8), :], -4 * p, 1)

    def z_sides(value, outer):
        up = roll(jnp.where(lane == 0, outer, value), -1, 1)
        down = roll(jnp.where(lane == 127, outer, value), 1, 1)
        return up, down

    def halo_row(ref, k, x):
        return jnp.broadcast_to(ref[pl.ds(k * NX + x, 1), :], (8, 128))

    def spread(ref, base, k, r):
        return ref[pl.ds(PAD + base + 64 * k + r, 8, stride=8), :]

    def fold(packed, send, count):
        def one(m, carry):
            even = packed[pl.ds(first(m * 16), 8), :]
            odd = packed[pl.ds(first(m * 16 + 8), 8), :]
            at = pl.ds(first(m * 8), 8)
            send[0, at, :] = jnp.where(low_half, even, roll(odd, 2, 1))
            send[1, at, :] = jnp.where(low_half, roll(odd, -2, 1), even)
            return carry
        lax.fori_loop(0, count * 4, one, 0)

    def z_pair(send, got, sems, sem_at):
        return [
            pltpu.make_async_remote_copy(
                src_ref=send.at[side], dst_ref=got.at[side], send_sem=sems[0].at[sem_at + side],
                recv_sem=sems[1].at[sem_at + side], device_id=(to, gy), device_id_type=MESH)
            for side, to in ((0, znext), (1, zprev))
        ]

    def y_pair(send, got, sems, sem_at):
        return [
            pltpu.make_async_remote_copy(
                src_ref=send.at[side], dst_ref=got.at[side], send_sem=sems[0].at[sem_at + side],
                recv_sem=sems[1].at[sem_at + side], device_id=(gz, to), device_id_type=MESH)
            for side, to in ((0, ynext), (1, yprev))
        ]

    def combine(got, pad, count):
        def one(m, carry):
            at = pl.ds(first(m * 8), 8)
            below, above = got[0, at, :], got[1, at, :]
            pad[pl.ds(first(m * 16), 8), :] = jnp.where(low_half, below, above)
            pad[pl.ds(first(m * 16 + 8), 8), :] = jnp.where(low_half, roll(below, -2, 1), roll(above, 2, 1))
            return carry
        lax.fori_loop(0, count * 4, one, 0)

    loads[0].wait()
    loads[1].wait()

    def widen(k, carry):
        at = pl.ds(pl.multiple_of(k * 64, 64), 64)
        to = pl.ds(first(PAD + k * 64), 64)
        tf[to, :] = tb[at, :].astype(jnp.float32)
        df[to, :] = db[at, :].astype(jnp.float32)
        return carry

    lax.fori_loop(0, NR // 64, widen, 0)

    def state_rows(k, carry):
        at = pl.ds(first(8 * k), 8)
        also = pl.ds(first(NX + 8 * k), 8)
        tysend[0, at, :] = spread(tf, 0, k, 7)
        tysend[0, also, :] = spread(df, 0, k, 7)
        tysend[1, at, :] = spread(tf, 0, k, 0)
        tysend[1, also, :] = spread(df, 0, k, 0)
        return carry

    lax.fori_loop(0, NX // 8, state_rows, 0)
    for c in range(3):
        loads[2 + c].wait()
    for load in loads[5:] + fetches:
        load.start()
    sources = [(tf, 0), (df, 0), (inc, 0), (inc, 1), (inc, 2)]

    def inner_rows(n, carry):
        c, k = n // 32, lax.rem(n, 32)
        at = pl.ds(first(8 * k), 8)
        rims[0, c, 1, at, :] = spread(inc, c * NR, k, 7)
        rims[1, c, 1, at, :] = spread(inc, c * NR, k, 0)
        return carry

    def outer_rows(n, carry):
        c, k = n // 32, lax.rem(n, 32)
        at = pl.ds(first(8 * k), 8)
        rims[0, c, 0, at, :] = -(spread(inc, c * NR, k, 6) + 2.0 * spread(w, c * NR, k, 7))
        rims[1, c, 0, at, :] = -(spread(inc, c * NR, k, 1) + 2.0 * spread(w, c * NR, k, 0))
        return carry

    rim_copies = {
        (c, kind): [
            pltpu.make_async_remote_copy(
                src_ref=rims.at[side, c, kind], dst_ref=rim_in.at[side, c, kind],
                send_sem=rs.at[side * 6 + c * 2 + kind], recv_sem=rr.at[side * 6 + c * 2 + kind],
                device_id=(gz, to), device_id_type=MESH)
            for side, to in ((0, ynext), (1, yprev))
        ]
        for c in range(3) for kind in range(2)
    }

    def begin_rims(*which):
        for one in which:
            for copy in rim_copies[one]:
                copy.start()

    lax.fori_loop(0, 96, inner_rows, 0)

    def pack_inputs(k, carry):
        for f, (ref, c) in enumerate(sources):
            acc = jnp.zeros((8, 128), jnp.float32)
            for p in range(PACK):
                acc = pack_into(acc, plane(ref, c, PACK * k + p), p)
            zsend[pl.ds(first(f * 64 + k * 8), 8), :] = acc
        return carry

    lax.fori_loop(0, packs, pack_inputs, 0)
    fold(zsend, zout, 5)
    pl.semaphore_wait(barrier, GY * GZ - 1)
    state_copies = y_pair(tysend, tyfrom, (ys, yr), 0)
    edge_copies = z_pair(zout, zfrom, (zs, zr), 0)
    for copy in edge_copies + state_copies:
        copy.start()

    for copy in edge_copies:
        copy.wait_recv()
    combine(zfrom, zpad, 5)

    def edge_laplacian(n, carry):
        c, k = n // 8, lax.rem(n, 8)
        base = 128 + c * 64

        def tile(ref, m):
            return ref[pl.ds(first(base + m * 8), 8), :]

        here, own = tile(zpad, k), tile(zsend, k)
        before, after = tile(zpad, lax.rem(k + 7, 8)), tile(zpad, lax.rem(k + 1, 8))
        x_down = jnp.where(slot == 0, roll(before, 4, 1), roll(here, 4, 1))
        x_up = jnp.where(slot == PACK - 1, roll(after, -4, 1), roll(here, -4, 1))
        y_sum = jnp.where(row == 7, 0.0, roll(here, -1, 0)) + jnp.where(row == 0, 0.0, roll(here, 1, 0))
        z_sum = jnp.where(low_half, roll(here, 1, 1) + roll(own, -1, 1), roll(here, -1, 1) + roll(own, 1, 1))
        wpad[pl.ds(first(c * 64 + k * 8), 8), :] = 6.0 * here - (x_down + x_up) - y_sum - z_sum
        return carry

    lax.fori_loop(0, 24, edge_laplacian, 0)

    def y_sum_closed(ref, c, x, beyond):
        return jnp.where(row == 7, beyond, y_up(ref, c, x)) + jnp.where(row == 0, beyond, y_down(ref, c, x))

    def laplacian(n, carry):
        c, k = n // packs, lax.rem(n, packs)
        cells = walk(inc, c, k)
        for i in range(PACK // GROUP):
            sum_u = jnp.zeros((8, 128), jnp.float32)
            sum_w = jnp.zeros((8, 128), jnp.float32)
            for p in range(GROUP * i, GROUP * i + GROUP):
                x = PACK * k + p
                before, u, after = next(cells)
                up, down = z_sides(u, unpacked(zpad, 2 + c, k, p))
                lap = 6.0 * u - (before + after) - y_sum_closed(inc, c, x, 0.0) - (up + down)
                put(w, c, x, lap)
                sum_u = sum_u + u
                sum_w = sum_w + lap
            at = pl.ds(first(c * 512 + k * 64 + i * 8), 8)
            su[at, :] = sum_u
            sw[at, :] = sum_w
        return carry

    lax.fori_loop(0, packs, laplacian, 0)

    for copy in state_copies:
        copy.wait_recv()

    begin_rims((0, 1))

    def differences(ref, field, k, keep_y, keep_z):
        for p, (before, here, after) in enumerate(walk(ref, 0, k)):
            x = PACK * k + p
            z_up, z_down = z_sides(here, unpacked(zpad, field, k, p))
            up = jnp.where(row == 7, halo_row(tyfrom.at[1], field, x), y_up(ref, 0, x))
            down = jnp.where(row == 0, halo_row(tyfrom.at[0], field, x), y_down(ref, 0, x))
            dy, dz = up - down, z_up - z_down
            put(keep_y, 0, x, dy)
            put(keep_z, 0, x, dz)
            yield after - before, dy, dz

    def first_state(k, carry):
        acc = jnp.zeros((8, 128), jnp.float32)
        for p, (dx, dy, dz) in enumerate(differences(tf, 0, k, g0y, g0z)):
            x = PACK * k + p
            value = -0.25 * (plane(inc, 0, x) * dx + plane(inc, 1, x) * dy + plane(inc, 2, x) * dz)
            put(s1, 0, x, value)
            acc = pack_into(acc, value, p)
        ssend[pl.ds(first(k * 8), 8), :] = acc
        return carry

    lax.fori_loop(0, packs, first_state, 0)
    fold(ssend, sout, 1)

    def s1_rows(k, carry):
        at = pl.ds(first(8 * k), 8)
        sysend[0, at, :] = spread(s1, 0, k, 7)
        sysend[1, at, :] = spread(s1, 0, k, 0)
        return carry

    lax.fori_loop(0, NX // 8, s1_rows, 0)
    s1_copies = z_pair(sout, sfrom, (zs, zr), 2) + y_pair(sysend, syfrom, (ys, yr), 2)
    for copy in s1_copies:
        copy.start()


    def fine(n, carry):
        c, k = n // packs, lax.rem(n, packs)
        for p, (before, lap, after) in enumerate(walk(w, c, k)):
            x = PACK * k + p
            u = plane(inc, c, x)
            up, down = z_sides(lap, unpacked(wpad, c, k, p))
            twice = 6.0 * lap - (before + after) - y_sum_closed(w, c, x, -u) - (up + down)
            put(hs, c, x, (OMEGA * GAMMA) * u + (OMEGA * BETA) * twice)
        return carry

    lax.fori_loop(packs, 3 * packs, laplacian, 0)
    lax.fori_loop(0, packs, fine, 0)

    for c in range(3):
        loads[5 + c].wait()
    for copy in s1_copies:
        copy.wait_recv()
    begin_rims((1, 1), (2, 1))
    combine(sfrom, spad, 1)

    def second_state(k, carry):
        acc = jnp.zeros((8, 128), jnp.float32)
        both = zip(differences(df, 1, k, g1y, g1z), walk(s1, 0, k))
        for p, ((dx, dy, dz), (s_before, s, s_after)) in enumerate(both):
            x = PACK * k + p
            z_up, z_down = z_sides(s, unpacked(spad, 0, k, p))
            up = jnp.where(row == 7, halo_row(syfrom.at[1], 0, x), y_up(s1, 0, x))
            down = jnp.where(row == 0, halo_row(syfrom.at[0], 0, x), y_down(s1, 0, x))
            moved = 0.5 * (plane(inc, 0, x) * dx + plane(inc, 1, x) * dy + plane(inc, 2, x) * dz)
            speed = None
            for c, (after, before) in enumerate(((s_after, s_before), (up, down), (z_up, z_down))):
                speed = plane(vel, c, x)
                moved = moved + jnp.maximum(speed, 0.0) * (s - before) + jnp.minimum(speed, 0.0) * (after - s)
            value = 0.5 * moved - s
            put(a2, 0, x, value)
            sent = jnp.where(lane >= 64, jnp.minimum(speed, 0.0), jnp.maximum(speed, 0.0)) * value
            acc = pack_into(acc, sent, p)
        qsend[pl.ds(first(k * 8), 8), :] = acc
        return carry

    lax.fori_loop(0, packs, second_state, 0)
    fold(qsend, qout, 1)

    def flux_rows(k, carry):
        at = pl.ds(first(8 * k), 8)
        qysend[0, at, :] = jnp.minimum(spread(vel, NR, k, 7), 0.0) * spread(a2, 0, k, 7)
        qysend[1, at, :] = jnp.maximum(spread(vel, NR, k, 0), 0.0) * spread(a2, 0, k, 0)
        return carry

    lax.fori_loop(0, NX // 8, flux_rows, 0)
    flux_copies = z_pair(qout, qfrom, (zs, zr), 4) + y_pair(qysend, qyfrom, (ys, yr), 4)
    for copy in flux_copies:
        copy.start()
    lax.fori_loop(0, 96, outer_rows, 0)
    lax.fori_loop(packs, 3 * packs, fine, 0)
    for copy in flux_copies:
        copy.wait_recv()
    begin_rims((0, 0))
    combine(qfrom, qpad, 1)

    def adjoint(k, carry):
        sums = []
        fields = zip(walk(a2, 0, k), walk(vel, 0, k), walk(tf, 0, k), walk(df, 0, k))
        for p, (near_a, near_v, near_t, near_d) in enumerate(fields):
            x = PACK * k + p
            if p % GROUP == 0:
                sums = [jnp.zeros((8, 128), jnp.float32) for _ in range(3)]
            a = near_a[1]
            vy, vz = plane(vel, 1, x), plane(vel, 2, x)
            size = jnp.abs(near_v[1]) + jnp.abs(vy) + jnp.abs(vz)
            change = jnp.maximum(near_v[2], 0.0) * near_a[2]
            change = change - jnp.minimum(near_v[0], 0.0) * near_a[0] - size * a
            p_up = jnp.maximum(y_up(vel, 1, x), 0.0) * y_up(a2, 0, x)
            q_down = jnp.minimum(y_down(vel, 1, x), 0.0) * y_down(a2, 0, x)
            change = change + jnp.where(row == 7, halo_row(qyfrom.at[1], 0, x), p_up)
            change = change - jnp.where(row == 0, halo_row(qyfrom.at[0], 0, x), q_down)
            qz, pz = jnp.minimum(vz, 0.0) * a, jnp.maximum(vz, 0.0) * a
            outer = unpacked(qpad, 0, k, p)
            change = change + roll(jnp.where(lane == 0, outer, pz), -1, 1)
            change = change - roll(jnp.where(lane == 127, outer, qz), 1, 1)
            scaled = (0.25 * OMEGA) * (a + 0.5 * change)
            other = (0.25 * OMEGA) * a
            pairs = (
                (near_t[2] - near_t[0], near_d[2] - near_d[0]),
                (plane(g0y, 0, x), plane(g1y, 0, x)),
                (plane(g0z, 0, x), plane(g1z, 0, x)),
            )
            for c, (from_t, from_d) in enumerate(pairs):
                value = plane(hs, c, x) + scaled * from_t + other * from_d
                put(hs, c, x, value)
                sums[c] = sums[c] + value
            if p % GROUP == GROUP - 1:
                for c in range(3):
                    sh[pl.ds(first(c * 512 + k * 64 + p // GROUP * 8), 8), :] = sums[c]
        return carry

    lax.fori_loop(0, packs, adjoint, 0)

    def rows_of(ref, c, r):
        return ref[pl.ds(c * 512 + r, CX, stride=8), :]

    for fetch in fetches:
        fetch.wait()

    def contribute():
        parts = []
        for c in range(3):
            scale = OMEGA * BETA
            parts.append(scale * (rows_of(su, c, 0) - rows_of(su, c, 1) - 2.0 * rows_of(sw, c, 0)))
            for half in (0, 4):
                parts.append(
                    (rows_of(sh, c, half) + rows_of(sh, c, half + 1))
                    + (rows_of(sh, c, half + 2) + rows_of(sh, c, half + 3)))
            parts.append(scale * (rows_of(su, c, 7) - rows_of(su, c, 6) - 2.0 * rows_of(sw, c, 7)))
        for c in range(3):
            lines = mm((fxh[...], fxl[...]), jnp.concatenate(parts[4 * c:4 * c + 4], axis=1))
            lines = mm(lines, (gather[...], None))
            for h in range(2):
                block = lines[h * GY:(h + 1) * GY]
                if c < 2:
                    fsend[h * GY:(h + 1) * GY, c, :] = block
                else:
                    fsend[(2 + h) * GY:(3 + h) * GY, 0, :] = block
                    fsend[(2 + h) * GY:(3 + h) * GY, 1, :] = block

    contribute()
    me = gz * GY + gy

    def exchange(send, got, ssem, rsem):
        def begin(k, z, y):
            pltpu.make_async_remote_copy(
                src_ref=send.at[z * GY + y], dst_ref=got.at[me], send_sem=ssem, recv_sem=rsem,
                device_id=(z, y), device_id_type=MESH).start()

        each_peer(begin)
        pltpu.make_async_copy(send.at[me], got.at[me], rsem).start()

        def finish():
            pltpu.make_async_copy(got, got, rsem).wait()

        def done():
            others = pl.ds(0, GY * GZ - 1)
            pltpu.make_async_copy(send.at[others], send.at[others], ssem).wait()

        return finish, done

    arrive, sent_forward = exchange(fsend, frecv, fs, fr)
    begin_rims((1, 0), (2, 0))
    total = eyz[...] + ex[pl.ds(2 * gy + lax.rem(gz, 2), 1), :]
    factor = (1.0 / (GAMMA + COARSE_BETA * total * total) - OMEGA) * (1.0 / (OMEGA * CX * CY * CZ))
    arrive()
    lane64 = lax.broadcasted_iota(jnp.int32, (CY, 128), 1) // 32
    lane32 = lax.broadcasted_iota(jnp.int32, (GY, 128), 1) // 32
    def solve():
        solved = []
        for s in range(2):
            whole = jnp.zeros((CY, 128), jnp.float32)
            for zb in range(GZ):
                lines = mm((fyh[...], fyl[...]), frecv[zb * GY:(zb + 1) * GY, s, :])
                merged = jnp.zeros((CY, 128), jnp.float32)
                for j in range(4):
                    moved = roll(lines[j * CY:(j + 1) * CY], 32 * (zb - j), 1)
                    merged = merged + moved
                whole = jnp.where(lane64 == zb, merged, whole)
            table_z = (bzh[...], bzl[...])
            modes = mm(whole, table_z) * factor
            solved.append(mm((iyh[...], iyl[...]), mm(modes, table_z)))
        for zb in range(GZ):
            block = jnp.zeros((GY, 128), jnp.float32)
            for s in range(2):
                for half in range(2):
                    part = roll(solved[s][half * GY:(half + 1) * GY], 32 * (2 * s + half - zb), 1)
                    block = jnp.where(lane32 == 2 * s + half, part, block)
            bsend[zb * GY:(zb + 1) * GY, 0, :] = block

    solve()
    arrive, sent_back = exchange(bsend, brecv, bs, br)
    arrive()
    def bring_back():
        for k in range(2):
            modes = brecv[2 * k * GY:(2 * k + 2) * GY, 0, :]
            lines = mm((ixh[...], ixl[...]), modes)
            count = 4 if k == 0 else 2
            wide = mm(lines, (spreader[:, :count * 128], None))
            for n in range(count):
                k_out[pl.ds((4 * k + n) * CX, CX), :] = wide[:, n * 128:(n + 1) * 128]

    bring_back()
    sent_forward()
    sent_back()
    for copy in edge_copies + state_copies + s1_copies + flux_copies:
        copy.wait_send()
    for pair in rim_copies.values():
        for copy in pair:
            copy.wait()


def finish(h_ref, rim_ref, k_ref, out_hbm, out, sems):
    row = lax.broadcasted_iota(jnp.int32, (8, 128), 0)
    planes = 64

    def copy(n):
        rows = pl.ds(pl.multiple_of(n * planes * 8, 8), planes * 8)
        return pltpu.make_async_copy(out.at[rows], out_hbm.at[rows], sems.at[n])

    def one(n, carry):
        c, part = n // (NX // planes), lax.rem(n, NX // planes)
        for p in range(planes):
            x = part * planes + p

            def wide(ref):
                return jnp.broadcast_to(ref[pl.ds(x, 1), :], (8, 128))

            rim = jnp.where(
                row < 4,
                *(jnp.broadcast_to(k_ref[pl.ds((2 * c + half) * CX + part * (planes // 4) + p // 4, 1), :], (8, 128))
                  for half in (0, 1)))
            late = jnp.zeros((8, 128), jnp.float32)
            for at, side, kind in ((0, 0, 0), (1, 0, 1), (6, 1, 1), (7, 1, 0)):
                late = jnp.where(row == at, wide(rim_ref.at[side, c, kind]), late)
            at = first((n * planes + p) * 8)
            out[pl.ds(at, 8), :] = h_ref[pl.ds(PAD + at, 8), :] + (rim + (OMEGA * BETA) * late)
        copy(n).start()
        return carry

    lax.fori_loop(0, 3 * NX // planes, one, 0)

    def drain(n, carry):
        copy(n).wait()
        return carry

    lax.fori_loop(0, 3 * NX // planes, drain, 0)


def per_device(velocity, increment, template, deformed):
    consts = [jnp.asarray(t) for t in tables()]
    f32 = jnp.float32
    vm = lambda *shape: pltpu.VMEM(shape, f32)
    dma = pltpu.SemaphoreType.DMA
    hessian, rims, coarse = pl.pallas_call(
        action,
        out_shape=(
            vm(3 * NR + 2 * PAD, 128),
            vm(2, 3, 2, NX, 128),
            vm(6 * CX, 128),
        ),
        in_specs=[pl.BlockSpec(memory_space=pltpu.HBM)] * (4 + len(consts)),
        out_specs=[pl.BlockSpec(memory_space=pltpu.VMEM)] * 3,
        scratch_shapes=[
            *[pltpu.VMEM(t.shape, t.dtype) for t in consts],
            vm(3 * NR + 2 * PAD, 128), vm(3 * NR + 2 * PAD, 128),
            pltpu.VMEM((NR, 128), jnp.bfloat16), pltpu.VMEM((NR, 128), jnp.bfloat16),
            *[vm(NR + 2 * PAD, 128)] * 4, vm(3 * NR + 2 * PAD, 128), *[vm(NR + 2 * PAD, 128)] * 4,
            vm(320, 128), vm(2, 160, 128), vm(2, 160, 128), vm(320, 128), vm(192, 128),
            *[vm(64, 128), vm(2, 32, 128), vm(2, 32, 128), vm(64, 128)] * 2,
            vm(2, 2 * NX, 128), vm(2, 2 * NX, 128), vm(2, NX, 128), vm(2, NX, 128), vm(2, NX, 128), vm(2, NX, 128),
            vm(2, 3, 2, NX, 128),
            vm(3 * 512, 128), vm(3 * 512, 128), vm(3 * 512, 128),
            vm(GZ * GY, 2, 128), vm(GZ * GY, 2, 128), vm(GZ * GY, 1, 128), vm(GZ * GY, 1, 128),
            dma((8,)), dma((6,)), dma((6,)), dma((6,)), dma((6,)), dma((12,)), dma((12,)),
            dma, dma, dma, dma, dma((TABLES,)),
        ],
        compiler_params=pltpu.CompilerParams(
            collective_id=1, has_side_effects=True, vmem_limit_bytes=40 * 1024 * 1024),
        name="action",
    )(
        *(pltpu.with_memory_space_constraint(x, pltpu.HBM) for x in (
            velocity.reshape(3 * NR, 128), increment.reshape(3 * NR, 128),
            template.reshape(NR, 128), deformed.reshape(NR, 128), *consts)),
    )
    result = pl.pallas_call(
        finish,
        out_shape=jax.ShapeDtypeStruct((3 * NR, 128), f32),
        in_specs=[pl.BlockSpec(memory_space=pltpu.VMEM)] * 3,
        out_specs=pl.BlockSpec(memory_space=pltpu.HBM),
        scratch_shapes=[vm(3 * NR, 128), dma((12,))],
        compiler_params=pltpu.CompilerParams(vmem_limit_bytes=16 * 1024 * 1024),
        name="finish",
    )(*(pltpu.with_memory_space_constraint(x, pltpu.VMEM) for x in (hessian, rims, coarse)))
    return result.reshape(3, NX, 8, 128)


def solution(mesh):
    placed = (
        P(None, None, "gy", "gz"),
        P(None, None, "gy", "gz"),
        P(None, "gy", "gz"),
        P(None, "gy", "gz"),
    )
    return jax.shard_map(
        per_device, mesh=mesh, in_specs=placed, out_specs=P(None, None, "gy", "gz"), check_vma=False
    )
```

```python
import functools
import math

import jax
import jax.numpy as jnp
import numpy as np
from jax import lax
from jax.experimental import pallas as pl
from jax.experimental.pallas import tpu as pltpu
from jax.sharding import PartitionSpec as P

MESH = pl.DeviceIdType.MESH
BETA = 0.02
GAMMA = 0.05
COARSE_BETA = 0.025
OMEGA = 1.0 / (0.05 + 42.0 * 0.02)

NX = 256
NR = NX * 8
GY = 32
GZ = 4
CX, CY, CZ = 64, 64, 128
PACK = 32
GROUP = 4
PAD = 8


def cas(rows, cols, count):
    angle = (np.outer(rows, cols) % count) * (2.0 * math.pi / count)
    return (np.cos(angle) + np.sin(angle)).astype(np.float32)


def eigen(count):
    return 2.0 - 2.0 * np.cos(np.arange(count) * (2.0 * math.pi / count))


def tables():
    owned = np.concatenate([2 * np.arange(GY), 2 * np.arange(GY) + 1])
    all_x, all_y, all_z = np.arange(CX), np.arange(CY), np.arange(CZ)
    forward_x = cas(owned, all_x, CX)
    inverse_x = cas(all_x, owned, CX)
    forward_y = np.concatenate([cas(all_y, (2 * np.arange(GY) - 1 + j) % CY, CY) for j in range(4)])
    inverse_y = cas(np.concatenate([2 * np.arange(GY), 2 * np.arange(GY) + 1]), all_y, CY)
    both_z = cas(all_z, all_z, CZ)
    gather_z = np.zeros((4 * 128, 128), np.float32)
    spread_z = np.zeros((128, 4 * 128), np.float32)
    for j in range(4):
        for z in range(128):
            gather_z[j * 128 + z, j * 32 + z // 4] = 1.0 / 64.0
            spread_z[j * 32 + z // 4, j * 128 + z] = 1.0
    eigen_yz = (eigen(CY)[:, None] + eigen(CZ)[None, :]).astype(np.float32)
    eigen_x = np.repeat(eigen(CX)[:, None], 128, axis=1).astype(np.float32)
    pairs = []
    for table in (forward_x, inverse_x, forward_y, inverse_y, both_z):
        high = table.astype(jnp.bfloat16)
        pairs += [high, (table - high.astype(np.float32)).astype(jnp.bfloat16)]
    return (*pairs, gather_z.astype(jnp.bfloat16), spread_z.astype(jnp.bfloat16), eigen_yz, eigen_x)


TABLES = 14


def halves(value):
    high = value.astype(jnp.bfloat16)
    return high, (value - high.astype(jnp.float32)).astype(jnp.bfloat16)


def mm(a, b):
    (ah, al), (bh, bl) = (x if isinstance(x, tuple) else halves(x) for x in (a, b))
    total = jnp.dot(ah, bh, preferred_element_type=jnp.float32)
    for x, y in ((ah, bl), (al, bh)):
        if x is not None and y is not None:
            total = total + jnp.dot(x, y, preferred_element_type=jnp.float32)
    return total


def first(x):
    return pl.multiple_of(x, 8)


def action(
    v_hbm, u_hbm, t_hbm, d_hbm,
    *refs,
):
    tables_hbm, refs = refs[:TABLES], refs[TABLES:]
    (hs, rim_in, k_out), refs = refs[:3], refs[3:]
    tables_vmem, refs = refs[:TABLES], refs[TABLES:]
    fxh, fxl, ixh, ixl, fyh, fyl, iyh, iyl, bzh, bzl, gather, spreader, eyz, ex = tables_vmem
    (
    vel, inc, tb, db, tf, df, s1, a2, w, g0y, g0z, g1y, g1z,
    zsend, zout, zfrom, zpad, wpad, ssend, sout, sfrom, spad, qsend, qout, qfrom, qpad,
    tysend, tyfrom, sysend, syfrom, qysend, qyfrom, rims,
    su, sw, sh, fsend, frecv, bsend, brecv,
    load_sem, zs, zr, ys, yr, rs, rr, fs, fr, bs, br,
        table_sem,
    ) = refs
    gz = lax.axis_index("gz")
    gy = lax.axis_index("gy")
    ynext, yprev = lax.rem(gy + 1, GY), lax.rem(gy + GY - 1, GY)
    znext, zprev = lax.rem(gz + 1, GZ), lax.rem(gz + GZ - 1, GZ)
    row = lax.broadcasted_iota(jnp.int32, (8, 128), 0)
    lane = lax.broadcasted_iota(jnp.int32, (8, 128), 1)
    slot = lax.rem(lax.shift_right_logical(lane + 2, 2), PACK)
    low_half = lax.rem(lane + 2, 4) < 2

    barrier = pltpu.get_barrier_semaphore()
    packs = NX // PACK

    def wrapped(k, count):
        return lax.select(k >= count, k - count, k)

    def each_peer(act):
        for kz in (2, 3, 1, 0):
            z = wrapped(gz + kz, GZ)

            def one(ky, carry):
                act(kz * GY + ky, z, wrapped(gy + ky, GY))
                return carry

            if kz == 0:
                for ky in range(1, 8):
                    one(ky, 0)
            lax.fori_loop(0 if kz else 8, GY, one, 0, unroll=8)

    def greet(k, z, y):
        pl.semaphore_signal(barrier, inc=1, device_id=(z, y), device_id_type=MESH)

    loads = [
        pltpu.make_async_copy(src, dst, load_sem.at[i])
        for i, (src, dst) in enumerate(
            [(t_hbm, tb), (d_hbm, db)]
            + [(u_hbm.at[pl.ds(c * NR, NR)], inc.at[pl.ds(PAD + c * NR, NR)]) for c in range(3)]
            + [(v_hbm.at[pl.ds(c * NR, NR)], vel.at[pl.ds(PAD + c * NR, NR)]) for c in range(3)]
        )
    ]
    fetches = [
        pltpu.make_async_copy(src, dst, table_sem.at[i]) for i, (src, dst) in enumerate(zip(tables_hbm, tables_vmem))
    ]
    for load in loads[:5]:
        load.start()
    each_peer(greet)

    def plane(ref, c, x):
        return ref[pl.ds(first(PAD + c * NR + x * 8), 8), :]

    def put(ref, c, x, value):
        ref[pl.ds(first(PAD + c * NR + x * 8), 8), :] = value

    def y_up(ref, c, x):
        return ref[pl.ds(PAD + 1 + c * NR + x * 8, 8), :]

    def y_down(ref, c, x):
        return ref[pl.ds(PAD - 1 + c * NR + x * 8, 8), :]

    def walk(ref, c, k):
        before = plane(ref, c, lax.rem(PACK * k + NX - 1, NX))
        here = plane(ref, c, PACK * k)
        for p in range(PACK):
            x = PACK * k + p + 1
            after = plane(ref, c, x if p < PACK - 1 else lax.rem(x, NX))
            yield before, here, after
            before, here = here, after

    def roll(value, shift, axis):
        return pltpu.roll(value, shift % value.shape[axis], axis)

    def pack_into(acc, value, p):
        return jnp.where(slot == p, roll(value, 4 * p, 1), acc)

    def unpacked(ref, f, k, p):
        return roll(ref[pl.ds(first(f * 64 + k * 8), 8), :], -4 * p, 1)

    def z_sides(value, outer):
        up = roll(jnp.where(lane == 0, outer, value), -1, 1)
        down = roll(jnp.where(lane == 127, outer, value), 1, 1)
        return up, down

    def halo_row(ref, k, x):
        return jnp.broadcast_to(ref[pl.ds(k * NX + x, 1), :], (8, 128))

    def spread(ref, base, k, r):
        return ref[pl.ds(PAD + base + 64 * k + r, 8, stride=8), :]

    def fold(packed, send, count):
        def one(m, carry):
            even = packed[pl.ds(first(m * 16), 8), :]
            odd = packed[pl.ds(first(m * 16 + 8), 8), :]
            at = pl.ds(first(m * 8), 8)
            send[0, at, :] = jnp.where(low_half, even, roll(odd, 2, 1))
            send[1, at, :] = jnp.where(low_half, roll(odd, -2, 1), even)
            return carry
        lax.fori_loop(0, count * 4, one, 0)

    def z_pair(send, got, sems, sem_at):
        return [
            pltpu.make_async_remote_copy(
                src_ref=send.at[side], dst_ref=got.at[side], send_sem=sems[0].at[sem_at + side],
                recv_sem=sems[1].at[sem_at + side], device_id=(to, gy), device_id_type=MESH)
            for side, to in ((0, znext), (1, zprev))
        ]

    def y_pair(send, got, sems, sem_at):
        return [
            pltpu.make_async_remote_copy(
                src_ref=send.at[side], dst_ref=got.at[side], send_sem=sems[0].at[sem_at + side],
                recv_sem=sems[1].at[sem_at + side], device_id=(gz, to), device_id_type=MESH)
            for side, to in ((0, ynext), (1, yprev))
        ]

    def combine(got, pad, count):
        def one(m, carry):
            at = pl.ds(first(m * 8), 8)
            below, above = got[0, at, :], got[1, at, :]
            pad[pl.ds(first(m * 16), 8), :] = jnp.where(low_half, below, above)
            pad[pl.ds(first(m * 16 + 8), 8), :] = jnp.where(low_half, roll(below, -2, 1), roll(above, 2, 1))
            return carry
        lax.fori_loop(0, count * 4, one, 0)

    loads[0].wait()
    loads[1].wait()

    def widen(k, carry):
        at = pl.ds(pl.multiple_of(k * 64, 64), 64)
        to = pl.ds(first(PAD + k * 64), 64)
        tf[to, :] = tb[at, :].astype(jnp.float32)
        df[to, :] = db[at, :].astype(jnp.float32)
        return carry

    lax.fori_loop(0, NR // 64, widen, 0)

    def state_rows(k, carry):
        at = pl.ds(first(8 * k), 8)
        also = pl.ds(first(NX + 8 * k), 8)
        tysend[0, at, :] = spread(tf, 0, k, 7)
        tysend[0, also, :] = spread(df, 0, k, 7)
        tysend[1, at, :] = spread(tf, 0, k, 0)
        tysend[1, also, :] = spread(df, 0, k, 0)
        return carry

    lax.fori_loop(0, NX // 8, state_rows, 0)
    for c in range(3):
        loads[2 + c].wait()
    for load in loads[5:] + fetches:
        load.start()
    sources = [(tf, 0), (df, 0), (inc, 0), (inc, 1), (inc, 2)]

    def inner_rows(n, carry):
        c, k = n // 32, lax.rem(n, 32)
        at = pl.ds(first(8 * k), 8)
        rims[0, c, 1, at, :] = spread(inc, c * NR, k, 7)
        rims[1, c, 1, at, :] = spread(inc, c * NR, k, 0)
        return carry

    def outer_rows(n, carry):
        c, k = n // 32, lax.rem(n, 32)
        at = pl.ds(first(8 * k), 8)
        rims[0, c, 0, at, :] = -(spread(inc, c * NR, k, 6) + 2.0 * spread(w, c * NR, k, 7))
        rims[1, c, 0, at, :] = -(spread(inc, c * NR, k, 1) + 2.0 * spread(w, c * NR, k, 0))
        return carry

    rim_copies = {
        (c, kind): [
            pltpu.make_async_remote_copy(
                src_ref=rims.at[side, c, kind], dst_ref=rim_in.at[side, c, kind],
                send_sem=rs.at[side * 6 + c * 2 + kind], recv_sem=rr.at[side * 6 + c * 2 + kind],
                device_id=(gz, to), device_id_type=MESH)
            for side, to in ((0, ynext), (1, yprev))
        ]
        for c in range(3) for kind in range(2)
    }

    def begin_rims(*which):
        for one in which:
            for copy in rim_copies[one]:
                copy.start()

    lax.fori_loop(0, 96, inner_rows, 0)

    def pack_inputs(k, carry):
        for f, (ref, c) in enumerate(sources):
            acc = jnp.zeros((8, 128), jnp.float32)
            for p in range(PACK):
                acc = pack_into(acc, plane(ref, c, PACK * k + p), p)
            zsend[pl.ds(first(f * 64 + k * 8), 8), :] = acc
        return carry

    lax.fori_loop(0, packs, pack_inputs, 0)
    fold(zsend, zout, 5)
    pl.semaphore_wait(barrier, GY * GZ - 1)
    state_copies = y_pair(tysend, tyfrom, (ys, yr), 0)
    edge_copies = z_pair(zout, zfrom, (zs, zr), 0)
    for copy in edge_copies + state_copies:
        copy.start()

    for copy in edge_copies:
        copy.wait_recv()
    combine(zfrom, zpad, 5)

    def edge_laplacian(n, carry):
        c, k = n // 8, lax.rem(n, 8)
        base = 128 + c * 64

        def tile(ref, m):
            return ref[pl.ds(first(base + m * 8), 8), :]

        here, own = tile(zpad, k), tile(zsend, k)
        before, after = tile(zpad, lax.rem(k + 7, 8)), tile(zpad, lax.rem(k + 1, 8))
        x_down = jnp.where(slot == 0, roll(before, 4, 1), roll(here, 4, 1))
        x_up = jnp.where(slot == PACK - 1, roll(after, -4, 1), roll(here, -4, 1))
        y_sum = jnp.where(row == 7, 0.0, roll(here, -1, 0)) + jnp.where(row == 0, 0.0, roll(here, 1, 0))
        z_sum = jnp.where(low_half, roll(here, 1, 1) + roll(own, -1, 1), roll(here, -1, 1) + roll(own, 1, 1))
        wpad[pl.ds(first(c * 64 + k * 8), 8), :] = 6.0 * here - (x_down + x_up) - y_sum - z_sum
        return carry

    lax.fori_loop(0, 24, edge_laplacian, 0)

    def y_sum_closed(ref, c, x, beyond):
        return jnp.where(row == 7, beyond, y_up(ref, c, x)) + jnp.where(row == 0, beyond, y_down(ref, c, x))

    def laplacian(n, carry):
        c, k = n // packs, lax.rem(n, packs)
        cells = walk(inc, c, k)
        for i in range(PACK // GROUP):
            sum_u = jnp.zeros((8, 128), jnp.float32)
            sum_w = jnp.zeros((8, 128), jnp.float32)
            for p in range(GROUP * i, GROUP * i + GROUP):
                x = PACK * k + p
                before, u, after = next(cells)
                up, down = z_sides(u, unpacked(zpad, 2 + c, k, p))
                lap = 6.0 * u - (before + after) - y_sum_closed(inc, c, x, 0.0) - (up + down)
                put(w, c, x, lap)
                sum_u = sum_u + u
                sum_w = sum_w + lap
            at = pl.ds(first(c * 512 + k * 64 + i * 8), 8)
            su[at, :] = sum_u
            sw[at, :] = sum_w
        return carry

    lax.fori_loop(0, packs, laplacian, 0)

    for copy in state_copies:
        copy.wait_recv()

    begin_rims((0, 1))

    def differences(ref, field, k, keep_y, keep_z):
        for p, (before, here, after) in enumerate(walk(ref, 0, k)):
            x = PACK * k + p
            z_up, z_down = z_sides(here, unpacked(zpad, field, k, p))
            up = jnp.where(row == 7, halo_row(tyfrom.at[1], field, x), y_up(ref, 0, x))
            down = jnp.where(row == 0, halo_row(tyfrom.at[0], field, x), y_down(ref, 0, x))
            dy, dz = up - down, z_up - z_down
            put(keep_y, 0, x, dy)
            put(keep_z, 0, x, dz)
            yield after - before, dy, dz

    def first_state(k, carry):
        acc = jnp.zeros((8, 128), jnp.float32)
        for p, (dx, dy, dz) in enumerate(differences(tf, 0, k, g0y, g0z)):
            x = PACK * k + p
            value = -0.25 * (plane(inc, 0, x) * dx + plane(inc, 1, x) * dy + plane(inc, 2, x) * dz)
            put(s1, 0, x, value)
            acc = pack_into(acc, value, p)
        ssend[pl.ds(first(k * 8), 8), :] = acc
        return carry

    lax.fori_loop(0, packs, first_state, 0)
    fold(ssend, sout, 1)

    def s1_rows(k, carry):
        at = pl.ds(first(8 * k), 8)
        sysend[0, at, :] = spread(s1, 0, k, 7)
        sysend[1, at, :] = spread(s1, 0, k, 0)
        return carry

    lax.fori_loop(0, NX // 8, s1_rows, 0)
    s1_copies = z_pair(sout, sfrom, (zs, zr), 2) + y_pair(sysend, syfrom, (ys, yr), 2)
    for copy in s1_copies:
        copy.start()


    def fine(n, carry):
        c, k = n // packs, lax.rem(n, packs)
        for p, (before, lap, after) in enumerate(walk(w, c, k)):
            x = PACK * k + p
            u = plane(inc, c, x)
            up, down = z_sides(lap, unpacked(wpad, c, k, p))
            twice = 6.0 * lap - (before + after) - y_sum_closed(w, c, x, -u) - (up + down)
            put(hs, c, x, (OMEGA * GAMMA) * u + (OMEGA * BETA) * twice)
        return carry

    lax.fori_loop(packs, 3 * packs, laplacian, 0)
    lax.fori_loop(0, packs, fine, 0)

    for c in range(3):
        loads[5 + c].wait()
    for copy in s1_copies:
        copy.wait_recv()
    begin_rims((1, 1), (2, 1))
    combine(sfrom, spad, 1)

    def second_state(k, carry):
        acc = jnp.zeros((8, 128), jnp.float32)
        both = zip(differences(df, 1, k, g1y, g1z), walk(s1, 0, k))
        for p, ((dx, dy, dz), (s_before, s, s_after)) in enumerate(both):
            x = PACK * k + p
            z_up, z_down = z_sides(s, unpacked(spad, 0, k, p))
            up = jnp.where(row == 7, halo_row(syfrom.at[1], 0, x), y_up(s1, 0, x))
            down = jnp.where(row == 0, halo_row(syfrom.at[0], 0, x), y_down(s1, 0, x))
            moved = 0.5 * (plane(inc, 0, x) * dx + plane(inc, 1, x) * dy + plane(inc, 2, x) * dz)
            speed = None
            for c, (after, before) in enumerate(((s_after, s_before), (up, down), (z_up, z_down))):
                speed = plane(vel, c, x)
                moved = moved + jnp.maximum(speed, 0.0) * (s - before) + jnp.minimum(speed, 0.0) * (after - s)
            value = 0.5 * moved - s
            put(a2, 0, x, value)
            sent = jnp.where(lane >= 64, jnp.minimum(speed, 0.0), jnp.maximum(speed, 0.0)) * value
            acc = pack_into(acc, sent, p)
        qsend[pl.ds(first(k * 8), 8), :] = acc
        return carry

    lax.fori_loop(0, packs, second_state, 0)
    fold(qsend, qout, 1)

    def flux_rows(k, carry):
        at = pl.ds(first(8 * k), 8)
        qysend[0, at, :] = jnp.minimum(spread(vel, NR, k, 7), 0.0) * spread(a2, 0, k, 7)
        qysend[1, at, :] = jnp.maximum(spread(vel, NR, k, 0), 0.0) * spread(a2, 0, k, 0)
        return carry

    lax.fori_loop(0, NX // 8, flux_rows, 0)
    flux_copies = z_pair(qout, qfrom, (zs, zr), 4) + y_pair(qysend, qyfrom, (ys, yr), 4)
    for copy in flux_copies:
        copy.start()
    lax.fori_loop(0, 96, outer_rows, 0)
    lax.fori_loop(packs, 3 * packs, fine, 0)
    for copy in flux_copies:
        copy.wait_recv()
    begin_rims((0, 0))
    combine(qfrom, qpad, 1)

    def adjoint(k, carry):
        sums = []
        fields = zip(walk(a2, 0, k), walk(vel, 0, k), walk(tf, 0, k), walk(df, 0, k))
        for p, (near_a, near_v, near_t, near_d) in enumerate(fields):
            x = PACK * k + p
            if p % GROUP == 0:
                sums = [jnp.zeros((8, 128), jnp.float32) for _ in range(3)]
            a = near_a[1]
            vy, vz = plane(vel, 1, x), plane(vel, 2, x)
            size = jnp.abs(near_v[1]) + jnp.abs(vy) + jnp.abs(vz)
            change = jnp.maximum(near_v[2], 0.0) * near_a[2]
            change = change - jnp.minimum(near_v[0], 0.0) * near_a[0] - size * a
            p_up = jnp.maximum(y_up(vel, 1, x), 0.0) * y_up(a2, 0, x)
            q_down = jnp.minimum(y_down(vel, 1, x), 0.0) * y_down(a2, 0, x)
            change = change + jnp.where(row == 7, halo_row(qyfrom.at[1], 0, x), p_up)
            change = change - jnp.where(row == 0, halo_row(qyfrom.at[0], 0, x), q_down)
            qz, pz = jnp.minimum(vz, 0.0) * a, jnp.maximum(vz, 0.0) * a
            outer = unpacked(qpad, 0, k, p)
            change = change + roll(jnp.where(lane == 0, outer, pz), -1, 1)
            change = change - roll(jnp.where(lane == 127, outer, qz), 1, 1)
            scaled = (0.25 * OMEGA) * (a + 0.5 * change)
            other = (0.25 * OMEGA) * a
            pairs = (
                (near_t[2] - near_t[0], near_d[2] - near_d[0]),
                (plane(g0y, 0, x), plane(g1y, 0, x)),
                (plane(g0z, 0, x), plane(g1z, 0, x)),
            )
            for c, (from_t, from_d) in enumerate(pairs):
                value = plane(hs, c, x) + scaled * from_t + other * from_d
                put(hs, c, x, value)
                sums[c] = sums[c] + value
            if p % GROUP == GROUP - 1:
                for c in range(3):
                    sh[pl.ds(first(c * 512 + k * 64 + p // GROUP * 8), 8), :] = sums[c]
        return carry

    lax.fori_loop(0, packs, adjoint, 0)

    def rows_of(ref, c, r):
        return ref[pl.ds(c * 512 + r, CX, stride=8), :]

    for fetch in fetches:
        fetch.wait()

    def contribute():
        parts = []
        for c in range(3):
            scale = OMEGA * BETA
            parts.append(scale * (rows_of(su, c, 0) - rows_of(su, c, 1) - 2.0 * rows_of(sw, c, 0)))
            for half in (0, 4):
                parts.append(
                    (rows_of(sh, c, half) + rows_of(sh, c, half + 1))
                    + (rows_of(sh, c, half + 2) + rows_of(sh, c, half + 3)))
            parts.append(scale * (rows_of(su, c, 7) - rows_of(su, c, 6) - 2.0 * rows_of(sw, c, 7)))
        for c in range(3):
            lines = mm((fxh[...], fxl[...]), jnp.concatenate(parts[4 * c:4 * c + 4], axis=1))
            lines = mm(lines, (gather[...], None))
            for h in range(2):
                block = lines[h * GY:(h + 1) * GY]
                if c < 2:
                    fsend[h * GY:(h + 1) * GY, c, :] = block
                else:
                    fsend[(2 + h) * GY:(3 + h) * GY, 0, :] = block
                    fsend[(2 + h) * GY:(3 + h) * GY, 1, :] = block

    contribute()
    me = gz * GY + gy

    def exchange(send, got, ssem, rsem):
        def begin(k, z, y):
            pltpu.make_async_remote_copy(
                src_ref=send.at[z * GY + y], dst_ref=got.at[me], send_sem=ssem, recv_sem=rsem,
                device_id=(z, y), device_id_type=MESH).start()

        each_peer(begin)
        pltpu.make_async_copy(send.at[me], got.at[me], rsem).start()

        def finish():
            pltpu.make_async_copy(got, got, rsem).wait()

        def done():
            others = pl.ds(0, GY * GZ - 1)
            pltpu.make_async_copy(send.at[others], send.at[others], ssem).wait()

        return finish, done

    arrive, sent_forward = exchange(fsend, frecv, fs, fr)
    begin_rims((1, 0), (2, 0))
    total = eyz[...] + ex[pl.ds(2 * gy + lax.rem(gz, 2), 1), :]
    factor = (1.0 / (GAMMA + COARSE_BETA * total * total) - OMEGA) * (1.0 / (OMEGA * CX * CY * CZ))
    arrive()
    lane64 = lax.broadcasted_iota(jnp.int32, (CY, 128), 1) // 32
    lane32 = lax.broadcasted_iota(jnp.int32, (GY, 128), 1) // 32
    def solve():
        solved = []
        for s in range(2):
            whole = jnp.zeros((CY, 128), jnp.float32)
            for zb in range(GZ):
                lines = mm((fyh[...], fyl[...]), frecv[zb * GY:(zb + 1) * GY, s, :])
                merged = jnp.zeros((CY, 128), jnp.float32)
                for j in range(4):
                    moved = roll(lines[j * CY:(j + 1) * CY], 32 * (zb - j), 1)
                    merged = merged + moved
                whole = jnp.where(lane64 == zb, merged, whole)
            table_z = (bzh[...], bzl[...])
            modes = mm(whole, table_z) * factor
            solved.append(mm((iyh[...], iyl[...]), mm(modes, table_z)))
        for zb in range(GZ):
            block = jnp.zeros((GY, 128), jnp.float32)
            for s in range(2):
                for half in range(2):
                    part = roll(solved[s][half * GY:(half + 1) * GY], 32 * (2 * s + half - zb), 1)
                    block = jnp.where(lane32 == 2 * s + half, part, block)
            bsend[zb * GY:(zb + 1) * GY, 0, :] = block

    solve()
    arrive, sent_back = exchange(bsend, brecv, bs, br)
    arrive()
    def bring_back():
        for k in range(2):
            modes = brecv[2 * k * GY:(2 * k + 2) * GY, 0, :]
            lines = mm((ixh[...], ixl[...]), modes)
            count = 4 if k == 0 else 2
            wide = mm(lines, (spreader[:, :count * 128], None))
            for n in range(count):
                k_out[pl.ds((4 * k + n) * CX, CX), :] = wide[:, n * 128:(n + 1) * 128]

    bring_back()
    sent_forward()
    sent_back()
    for copy in edge_copies + state_copies + s1_copies + flux_copies:
        copy.wait_send()
    for pair in rim_copies.values():
        for copy in pair:
            copy.wait()


def finish(h_ref, rim_ref, k_ref, out_hbm, out, sems):
    row = lax.broadcasted_iota(jnp.int32, (8, 128), 0)
    planes = 64

    def copy(n):
        rows = pl.ds(pl.multiple_of(n * planes * 8, 8), planes * 8)
        return pltpu.make_async_copy(out.at[rows], out_hbm.at[rows], sems.at[n])

    def one(n, carry):
        c, part = n // (NX // planes), lax.rem(n, NX // planes)
        for p in range(planes):
            x = part * planes + p

            def wide(ref):
                return jnp.broadcast_to(ref[pl.ds(x, 1), :], (8, 128))

            rim = jnp.where(
                row < 4,
                *(jnp.broadcast_to(k_ref[pl.ds((2 * c + half) * CX + part * (planes // 4) + p // 4, 1), :], (8, 128))
                  for half in (0, 1)))
            late = jnp.zeros((8, 128), jnp.float32)
            for at, side, kind in ((0, 0, 0), (1, 0, 1), (6, 1, 1), (7, 1, 0)):
                late = jnp.where(row == at, wide(rim_ref.at[side, c, kind]), late)
            at = first((n * planes + p) * 8)
            out[pl.ds(at, 8), :] = h_ref[pl.ds(PAD + at, 8), :] + (rim + (OMEGA * BETA) * late)
        copy(n).start()
        return carry

    lax.fori_loop(0, 3 * NX // planes, one, 0)

    def drain(n, carry):
        copy(n).wait()
        return carry

    lax.fori_loop(0, 3 * NX // planes, drain, 0)


def per_device(velocity, increment, template, deformed):
    consts = [jnp.asarray(t) for t in tables()]
    f32 = jnp.float32
    vm = lambda *shape: pltpu.VMEM(shape, f32)
    dma = pltpu.SemaphoreType.DMA
    hessian, rims, coarse = pl.pallas_call(
        action,
        out_shape=(
            vm(3 * NR + 2 * PAD, 128),
            vm(2, 3, 2, NX, 128),
            vm(6 * CX, 128),
        ),
        in_specs=[pl.BlockSpec(memory_space=pltpu.HBM)] * (4 + len(consts)),
        out_specs=[pl.BlockSpec(memory_space=pltpu.VMEM)] * 3,
        scratch_shapes=[
            *[pltpu.VMEM(t.shape, t.dtype) for t in consts],
            vm(3 * NR + 2 * PAD, 128), vm(3 * NR + 2 * PAD, 128),
            pltpu.VMEM((NR, 128), jnp.bfloat16), pltpu.VMEM((NR, 128), jnp.bfloat16),
            *[vm(NR + 2 * PAD, 128)] * 4, vm(3 * NR + 2 * PAD, 128), *[vm(NR + 2 * PAD, 128)] * 4,
            vm(320, 128), vm(2, 160, 128), vm(2, 160, 128), vm(320, 128), vm(192, 128),
            *[vm(64, 128), vm(2, 32, 128), vm(2, 32, 128), vm(64, 128)] * 2,
            vm(2, 2 * NX, 128), vm(2, 2 * NX, 128), vm(2, NX, 128), vm(2, NX, 128), vm(2, NX, 128), vm(2, NX, 128),
            vm(2, 3, 2, NX, 128),
            vm(3 * 512, 128), vm(3 * 512, 128), vm(3 * 512, 128),
            vm(GZ * GY, 2, 128), vm(GZ * GY, 2, 128), vm(GZ * GY, 1, 128), vm(GZ * GY, 1, 128),
            dma((8,)), dma((6,)), dma((6,)), dma((6,)), dma((6,)), dma((12,)), dma((12,)),
            dma, dma, dma, dma, dma((TABLES,)),
        ],
        compiler_params=pltpu.CompilerParams(
            collective_id=1, has_side_effects=True, vmem_limit_bytes=40 * 1024 * 1024),
        name="action",
    )(
        *(pltpu.with_memory_space_constraint(x, pltpu.HBM) for x in (
            velocity.reshape(3 * NR, 128), increment.reshape(3 * NR, 128),
            template.reshape(NR, 128), deformed.reshape(NR, 128), *consts)),
    )
    result = pl.pallas_call(
        finish,
        out_shape=jax.ShapeDtypeStruct((3 * NR, 128), f32),
        in_specs=[pl.BlockSpec(memory_space=pltpu.VMEM)] * 3,
        out_specs=pl.BlockSpec(memory_space=pltpu.HBM),
        scratch_shapes=[vm(3 * NR, 128), dma((12,))],
        compiler_params=pltpu.CompilerParams(vmem_limit_bytes=16 * 1024 * 1024),
        name="finish",
    )(*(pltpu.with_memory_space_constraint(x, pltpu.VMEM) for x in (hessian, rims, coarse)))
    return result.reshape(3, NX, 8, 128)


def solution(mesh):
    placed = (
        P(None, None, "gy", "gz"),
        P(None, None, "gy", "gz"),
        P(None, "gy", "gz"),
        P(None, "gy", "gz"),
    )
    return jax.shard_map(
        per_device, mesh=mesh, in_specs=placed, out_specs=P(None, None, "gy", "gz"), check_vma=False
    )
```
